32 devices in a mesh: dp: 8 (over z, x), tensor: 4 (over y, core).
Axes of the slice: x: 2, y: 2, z: 4, core: 2. Of those that a mesh axis runs over, the one named last changes fastest.
Arguments:
- tokens: bfloat16 [16384, 768], P('dp'), may hold values from -6 to 6
- seq_lengths: int32 [8, 9], P('dp'), may hold values from 1 to 512, 2048 in all within a row
- query_weight: bfloat16 [768, 768], P(None, 'tensor'), may hold values from -0.21875 to 0.21875
- key_weight: bfloat16 [768, 768], P(None, 'tensor'), may hold values from -0.21875 to 0.21875
- value_weight: bfloat16 [768, 768], P(None, 'tensor'), may hold values from -0.21875 to 0.21875
- out_weight: bfloat16 [768, 768], P('tensor'), may hold values from -0.875 to 0.875
- ffn_in: bfloat16 [768, 3072], P(None, 'tensor'), may hold values from -0.21875 to 0.21875
- ffn_out: bfloat16 [3072, 768], P('tensor'), may hold values from -0.109375 to 0.109375
- gain_attn: float32 [768], replicated, may hold values from 0.5 to 1.5
- gain_ffn: float32 [768], replicated, may hold values from 0.5 to 1.5
- query_down: bfloat16 [768, 8], replicated, may hold values from -0.21875 to 0.21875
- value_down: bfloat16 [768, 8], replicated, may hold values from -0.21875 to 0.21875
- query_up: bfloat16 [8, 12, 64], P(None, 'tensor'), may hold values from -1.078125 to 1.078125
- value_up: bfloat16 [8, 12, 64], P(None, 'tensor'), may hold values from -1.078125 to 1.078125
- cotangent: bfloat16 [16384, 768], P('dp'), may hold values from -6 to 6
Outputs:
- activations: bfloat16 [16384, 768], P(('dp', 'tensor'))
- input_grad: float32 [16384, 768], P(('dp', 'tensor'))
- query_up_grad: float32 [8, 12, 64], P(None, 'tensor', 'dp')
- value_up_grad: float32 [8, 12, 64], P(None, 'tensor', 'dp')
The draws below stay inside these ranges and needn't reach their ends.
Inputs may be any that keep to these rules, and one draw needn't show every extreme that they name: `seq_lengths`: row b holds the lengths of the 8 sequences packed from the start of the b-th block of 2048 slots, in order, then the number of padding slots at the block's end; every row sums to 2048 and reaches 512.
All inputs are finite; a program needn't handle non-finite values.
Results may differ from the reference program's by a relative error of at most 0.025.
Values may be sent and summed in bfloat16 or wider, within the bound.
A program may use at most 128 MiB of HBM per device.

```python
import math
from functools import partial
import jax
import jax.numpy as jnp
import numpy as np
from jax import lax

D = 768
H = 12
HD = 64
FF = 3072
R = 8
SEQ = 512
TOK_DEV = 2048
SEQS_DEV = 8
TOKENS = 16384
N_DP = 8
N_TENSOR = 4


def steps_of(key, dims, shards, low, top_value):
    def one(dim, blocks):
        heights = jax.random.uniform(jax.random.fold_in(jax.random.fold_in(key, 6), dim), (blocks,), jnp.float32, low / len(shards), top_value / len(shards))
        return jnp.repeat(jnp.exp(heights), dims[dim] // blocks).reshape((-1,) + (1,) * (len(dims) - dim - 1))

    gain = one(*shards[0])
    for cut in shards[1:]:
        gain = gain * one(*cut)
    return gain


def profile(number_of, total, limit, lean):
    weights = [(1 << 20) // math.isqrt(standing ** lean) + 1 for standing in range(2, number_of + 1)]
    rest, holding = total - limit - (number_of - 1), [1] * (number_of - 1)
    while rest > 0:
        candidates = [i for i in range(number_of - 1) if holding[i] < limit]
        mass, remaining = sum([weights[i] for i in candidates]), rest
        for i in candidates:
            more = min(limit - holding[i], max(1, remaining * weights[i] // mass), rest)
            holding[i] = holding[i] + more
            rest = rest - more
    return np.array([limit] + holding)


def ragged_sizes(stream_key, amount, total, bound, lean):
    if amount == 2:
        one = jax.random.randint(stream_key, (), max(1, total - bound), min(bound, total - 1) + 1)
        return jnp.stack([one, total - one])
    tallies = jnp.asarray(profile(amount, total, bound, lean), jnp.int32)
    twos = (amount - 1) // 2
    donor, receiver = tallies[1:1 + 2 * twos:2], tallies[2:2 + 2 * twos:2]
    margin = jnp.minimum(donor - 1, bound - receiver)
    moved = jax.random.randint(jax.random.fold_in(stream_key, 1), (twos,), 0, 1 << 20) % (margin + 1)
    tallies = tallies.at[1:1 + 2 * twos:2].set(donor - moved).at[2:2 + 2 * twos:2].set(receiver + moved)
    return tallies[jax.random.permutation(jax.random.fold_in(stream_key, 2), amount)]


def normal_values(own_key, shape, width, limit, pieces=(), kind=jnp.bfloat16):
    level = steps_of(own_key, shape, pieces, -0.22, 0.18) if pieces else 1.0
    values = jax.random.normal(own_key, shape, jnp.float32) * width * level
    return jnp.minimum(jnp.maximum(values, -limit), limit).astype(kind)


def setup_inputs(seed: int = 0) -> dict:
    key_list = jax.random.split(jax.random.key(seed), 16)
    tokens = normal_values(key_list[0], (TOKENS, D), 1.0, 6.0, ((0, 8),))
    seq_lengths = jax.vmap(lambda own: ragged_sizes(own, SEQS_DEV + 1, TOK_DEV, SEQ, 2))(jax.random.split(key_list[1], N_DP)).reshape((N_DP, SEQS_DEV + 1)).astype(jnp.int32)
    query_weight = normal_values(key_list[2], (D, D), D ** -0.5, 0.21875, ((1, 4),))
    key_weight = normal_values(key_list[3], (D, D), D ** -0.5, 0.21875, ((1, 4),))
    value_weight = normal_values(key_list[4], (D, D), D ** -0.5, 0.21875, ((1, 4),))
    out_weight = normal_values(key_list[5], (D, D), (D // 16) ** -0.5, 0.875, ((0, 4),))
    ffn_in = normal_values(key_list[6], (D, FF), D ** -0.5, 0.21875, ((1, 4),))
    ffn_out = normal_values(key_list[7], (FF, D), FF ** -0.5, 0.109375, ((0, 4),))
    gain_attn = jnp.clip(1.0 + 0.1 * jax.random.normal(key_list[8], (D,), jnp.float32), 0.5, 1.5)
    gain_ffn = jnp.clip(1.0 + 0.1 * jax.random.normal(key_list[9], (D,), jnp.float32), 0.5, 1.5)
    query_down = normal_values(key_list[10], (D, R), D ** -0.5, 0.21875)
    value_down = normal_values(key_list[11], (D, R), D ** -0.5, 0.21875)
    query_up = normal_values(key_list[12], (R, H, HD), 0.18, 1.078125, ((1, 4),))
    value_up = normal_values(key_list[13], (R, H, HD), 0.18, 1.078125, ((1, 4),))
    cotangent = normal_values(key_list[14], (TOKENS, D), 1.0, 6.0, ((0, 8),))
    return dict(tokens=tokens, seq_lengths=seq_lengths, query_weight=query_weight, key_weight=key_weight, value_weight=value_weight, out_weight=out_weight, ffn_in=ffn_in, ffn_out=ffn_out, gain_attn=gain_attn, gain_ffn=gain_ffn, query_down=query_down, value_down=value_down, query_up=query_up, value_up=value_up, cotangent=cotangent)


EPSILON = 1e-05
NEGATIVE = -1e+30

@jax.custom_vjp
def low(v):
    return lax.optimization_barrier(v.astype(jnp.bfloat16)).astype(jnp.float32)

@jax.custom_vjp
def low_back(v):
    return v

def low_keep(v):
    return (low(v), None)

def low_pass(kept, grad):
    return (grad,)

def back_keep(v):
    return (v, None)

def back_low(kept, grad):
    return (low(grad),)
low.defvjp(low_keep, low_pass)
low_back.defvjp(back_keep, back_low)

def product(left_side, right_side):
    return jnp.dot(left_side, right_side, precision=lax.Precision.HIGHEST, preferred_element_type=jnp.float32)

def layer_norm(vector, scale_gain):
    average = lax.optimization_barrier(jnp.mean(vector, axis=-1, keepdims=True))
    centered = vector - average
    inverse = lax.rsqrt(lax.optimization_barrier(jnp.mean(centered * centered, axis=-1, keepdims=True)) + EPSILON)
    return centered * inverse * scale_gain

def head_attention(allowed, is_valid, head_parts):
    query_head, key_head, value_head = head_parts
    scores = low_back(product(query_head, key_head.T) * HD ** (-0.5))
    masked = jnp.where(allowed, scores, NEGATIVE)
    row_max = lax.optimization_barrier(jnp.max(masked, axis=-1, keepdims=True))
    weights = jnp.where(allowed, jnp.exp(masked - row_max), 0.0)
    row_total = lax.optimization_barrier(jnp.sum(weights, axis=-1, keepdims=True)) + (1.0 - is_valid)[:, None]
    probability = low(weights / row_total)
    return product(probability, value_head)

def split_heads(matrix):
    return matrix.reshape(matrix.shape[0], H, HD).transpose(1, 0, 2)

def shard_forward(inputs, up_query, up_value, frozen, allowed, is_valid):
    w_query, w_key, w_value, w_out, w_inner, w_ffn_out, gain_one, gain_two, down_query, down_value = frozen
    group_cols = D // N_TENSOR
    inner_cols = FF // N_TENSOR
    query_parts, key_parts, value_parts = ([], [], [])
    for group_index in range(N_TENSOR):
        copied = low_back(inputs)
        col_start = group_index * group_cols
        col_end = col_start + group_cols
        low_query = low(product(copied, down_query))
        low_value = low(product(copied, down_value))
        query_parts.append(product(copied, w_query[:, col_start:col_end]) + 2.0 * product(low_query, up_query[:, col_start:col_end]))
        key_parts.append(product(copied, w_key[:, col_start:col_end]))
        value_parts.append(product(copied, w_value[:, col_start:col_end]) + 2.0 * product(low_value, up_value[:, col_start:col_end]))
    queries = low(low_back(jnp.concatenate(query_parts, axis=1)))
    key_rows = low(low_back(jnp.concatenate(key_parts, axis=1)))
    values = low(low_back(jnp.concatenate(value_parts, axis=1)))
    attend = jax.checkpoint(partial(head_attention, allowed, is_valid))
    mixed_rows = lax.map(attend, (split_heads(queries), split_heads(key_rows), split_heads(values)))
    context = low(low_back(mixed_rows.transpose(1, 0, 2).reshape(inputs.shape[0], D)))
    attn_out = jnp.zeros_like(inputs)
    for group_index in range(N_TENSOR):
        col_start = group_index * group_cols
        col_end = col_start + group_cols
        attn_out = attn_out + low(product(context[:, col_start:col_end], w_out[col_start:col_end, :]))
    attn_out = low_back(attn_out)
    normed = layer_norm(inputs + attn_out, gain_one)
    normed_low = low(normed)
    ffn_result = jnp.zeros_like(inputs)
    for group_index in range(N_TENSOR):
        col_start = group_index * inner_cols
        col_end = col_start + inner_cols
        copied = low_back(normed_low)
        pre_act = low_back(product(copied, w_inner[:, col_start:col_end]))
        active = low(jax.nn.gelu(pre_act, approximate=False))
        ffn_result = ffn_result + low(product(active, w_ffn_out[col_start:col_end, :]))
    ffn_result = low_back(ffn_result)
    return layer_norm(normed + ffn_result, gain_two) * is_valid[:, None]

def reference(tokens, seq_lengths, query_weight, key_weight, value_weight, out_weight, ffn_in, ffn_out, gain_attn, gain_ffn, query_down, value_down, query_up, value_up, cotangent):
    frozen = tuple((weight_arg.astype(jnp.float32) for weight_arg in (query_weight, key_weight, value_weight, out_weight, ffn_in, ffn_out, gain_attn, gain_ffn, query_down, value_down)))
    up_query = query_up.astype(jnp.float32).reshape(R, D)
    up_value = value_up.astype(jnp.float32).reshape(R, D)
    token_blocks = tokens.astype(jnp.float32).reshape(N_DP, TOK_DEV, D)
    grad_blocks = cotangent.astype(jnp.float32).reshape(N_DP, TOK_DEV, D)
    positions = jnp.arange(TOK_DEV, dtype=jnp.int32)

    def shard_step(accumulated, shard_inputs):
        block_tokens, block_lengths, block_grads = shard_inputs
        seg_ends = jnp.cumsum(block_lengths)
        segment = lax.optimization_barrier(jnp.sum((positions[:, None] >= seg_ends[None, :]).astype(jnp.int32), axis=1))
        inside = segment < block_lengths.shape[0] - 1
        is_valid = inside.astype(jnp.float32)
        allowed = (segment[:, None] == segment[None, :]) & inside[:, None]

        def forward(inputs, first_up, second_up):
            return shard_forward(inputs, first_up, second_up, frozen, allowed, is_valid)
        result, pull = jax.vjp(forward, block_tokens, up_query, up_value)
        grad_input, grad_query, grad_value = pull(block_grads)
        return ((accumulated[0] + grad_query, accumulated[1] + grad_value), (result.astype(jnp.bfloat16), grad_input))
    empty_grad = jnp.zeros((R, D), jnp.float32)
    (grad_query, grad_value), (results, grad_inputs) = lax.scan(shard_step, (empty_grad, empty_grad), (token_blocks, seq_lengths, grad_blocks))
    return (results.reshape(TOKENS, D), grad_inputs.reshape(TOKENS, D), grad_query.reshape(R, H, HD), grad_value.reshape(R, H, HD))
```

```python
import functools

import jax
import jax.numpy as jnp
from jax import lax
from jax.experimental import pallas as pl
from jax.experimental.pallas import tpu as pltpu
from jax.sharding import PartitionSpec as P

EPSILON = 1e-05
BLOCKED = -1e30
LOG2E = 1.4426950408889634
BLK = 256
LANES = 128
f32 = jnp.float32
bf16 = jnp.bfloat16
VMEM_LIMIT = 64 * 1024 * 1024 - 65536


def dot(a, b):
    return jnp.dot(a, b, preferred_element_type=f32)


def dot_nt(a, b):
    return lax.dot_general(a, b, (((1,), (1,)), ((), ())), preferred_element_type=f32)


def lane_iota(rows, lanes=LANES):
    return lax.broadcasted_iota(jnp.int32, (rows, lanes), 1)


def selection(rows, lanes, target):
    r = lax.broadcasted_iota(jnp.int32, (rows, lanes), 0)
    c = lax.broadcasted_iota(jnp.int32, (rows, lanes), 1)
    return jnp.where(c == target(r), 1.0, 0.0).astype(bf16)


def three_parts(x):
    hi = x.astype(bf16).astype(f32)
    mid = (x - hi).astype(bf16).astype(f32)
    low = (x - hi - mid).astype(bf16).astype(f32)
    return hi, mid, low


def segment_bounds(len_ref, slots):
    starts, ends = [], []
    total = jnp.int32(0)
    for s in range(slots):
        starts.append(total)
        total = total + len_ref[0, s]
        ends.append(total)
    return starts, ends


def block_range(starts, ends, row0):
    first, last = jnp.int32(0), jnp.int32(0)
    for s, e in zip(starts, ends):
        first = jnp.where((s <= row0) & (row0 < e), s, first)
        edge = row0 + BLK - 1
        last = jnp.where((s <= edge) & (edge < e), e, last)
    return first // BLK, (last + BLK - 1) // BLK


def attend_kernel(heads, hd, len_ref, tok_ref, wq_ref, wk_ref, wv_ref, dq_ref, dv_ref, uq_ref, uv_ref,
                  qa_ref, ka_ref, va_ref, kt_ref, ctx_ref, lowt_ref, weff_ref,
                  wbig, up, scores, peak, total):
    rows = tok_ref.shape[0]
    width = heads * hd
    pad = heads * LANES
    slots = len_ref.shape[1]
    rank = dq_ref.shape[1]
    starts, ends = segment_bounds(len_ref, slots)

    spread = selection(width, pad, lambda r: (r // hd) * LANES + r % hd)
    wq, wk, wv = wq_ref[...], wk_ref[...], wv_ref[...]
    for i, w in enumerate((wq, wk, wv)):
        wbig[:, i * pad:(i + 1) * pad] = dot(w, spread).astype(bf16)
    low_q = selection(rank, LANES, lambda r: r)
    low_v = selection(rank, LANES, lambda r: r + rank)
    wbig[:, 3 * pad:] = (dot(dq_ref[...], low_q) + dot(dv_ref[...], low_v)).astype(bf16)
    uq, uv = uq_ref[...], uv_ref[...]
    up[...] = jnp.zeros_like(up)
    up[0:2 * rank, 0:pad] = dot(selection(2 * rank, rank, lambda r: r), 2.0 * dot(uq, spread).astype(bf16)).astype(bf16)
    up[0:2 * rank, pad:] = dot(selection(2 * rank, rank, lambda r: r - rank), 2.0 * dot(uv, spread).astype(bf16)).astype(bf16)
    pack = weff_ref.shape[1]
    weff_ref[...] = (
        dot((wq.astype(f32) + 2.0 * dot(dq_ref[...], uq)).astype(bf16), selection(width, pack, lambda r: r))
        + dot(wk, selection(width, pack, lambda r: r + width))
        + dot((wv.astype(f32) + 2.0 * dot(dv_ref[...], uv)).astype(bf16), selection(width, pack, lambda r: r + 2 * width))
    ).astype(bf16)

    lane = lane_iota(1)
    seg_start = jnp.zeros((1, LANES), jnp.int32)
    seg_end = jnp.zeros((1, LANES), jnp.int32)
    for s in range(slots):
        seg_start = jnp.where(lane == hd + s, starts[s], seg_start)
        seg_end = jnp.where(lane == hd + s, ends[s], seg_end)
    is_mask = (lane >= hd) & (lane < hd + slots)
    extra = (lane >= hd + slots) & (lane < hd + slots + 3)
    ones_v = jnp.where((lane >= hd) & (lane < hd + 3), 1.0, 0.0)

    def project(i, _):
        r0 = pl.multiple_of(i * BLK, BLK)
        span = pl.ds(r0, BLK)
        x = tok_ref[span, :]
        low = dot(x, wbig[:, 3 * pad:]).astype(bf16)
        lowt_ref[:, span] = low.astype(f32).T[0:2 * rank, :].astype(bf16)
        pos = r0 + lax.broadcasted_iota(jnp.int32, (BLK, LANES), 0)
        own = (pos >= seg_start) & (pos < seg_end)
        q_mask = jnp.where(own, 1.0, 0.0)
        k_mask = jnp.where(is_mask & jnp.logical_not(own), BLOCKED, jnp.where(extra, 1.0, 0.0))
        q = dot(x, wbig[:, 0:pad]) + dot(low, up[:, 0:pad])
        for h in range(heads):
            qh = q[:, h * LANES:(h + 1) * LANES].astype(bf16).astype(f32)
            qa_ref[h, span, :] = (qh * hd ** -0.5 + q_mask).astype(bf16)
        k = dot(x, wbig[:, pad:2 * pad])
        for h in range(heads):
            kh = k[:, h * LANES:(h + 1) * LANES]
            ka_ref[h, span, :] = (kh + k_mask).astype(bf16)
            kt_ref[h, :, span] = kh.T[0:hd, :].astype(bf16)
        v = dot(x, wbig[:, 2 * pad:3 * pad]) + dot(low, up[:, pad:])
        for h in range(heads):
            va_ref[h, span, :] = (v[:, h * LANES:(h + 1) * LANES] + ones_v).astype(bf16)
        return 0

    lax.fori_loop(0, rows // BLK, project, 0)

    lanes = lane_iota(BLK)
    group = ctx_ref.shape[1] * 2 // 3

    def attend(g, half):
        per = group // BLK
        row0 = pl.multiple_of(g * group + half * BLK, BLK)
        span = pl.ds(row0, BLK)
        lo, hi = block_range(starts, ends, row0)
        peak[...] = jnp.full(peak.shape, BLOCKED, f32)
        total[...] = jnp.zeros_like(total)

        def first(kb, _):
            keys = pl.ds(pl.multiple_of(kb * BLK, BLK), BLK)
            for h in range(heads):
                s = dot_nt(qa_ref[h, span, :], ka_ref[h, keys, :])
                scores[h, kb - lo] = s
                best = peak[h]
                for c in range(BLK // LANES):
                    best = jnp.maximum(best, s[:, c * LANES:(c + 1) * LANES])
                peak[h] = best
            return 0

        lax.fori_loop(lo, hi, first, 0)
        for h in range(heads):
            peak[h] = jnp.broadcast_to(jnp.max(peak[h], axis=1, keepdims=True), (BLK, LANES))

        def second(kb, _):
            keys = pl.ds(pl.multiple_of(kb * BLK, BLK), BLK)
            for h in range(heads):
                top = jnp.concatenate([peak[h]] * (BLK // LANES), axis=1)
                p = jnp.exp2((scores[h, kb - lo] - top) * LOG2E).astype(bf16)
                total[h] += dot(p, va_ref[h, keys, :])
            return 0

        lax.fori_loop(lo, hi, second, 0)
        outs = []
        for h in range(heads):
            acc = total[h]
            norm = jnp.broadcast_to(acc[:, hd:hd + 1], (BLK, LANES))
            outs.append(acc / norm)
            hi_p, mid_p, low_p = three_parts(-(peak[h] + jnp.log(norm)))
            old = qa_ref[h, span, :].astype(f32)
            new = jnp.where(lanes == hd + slots, hi_p, old)
            new = jnp.where(lanes == hd + slots + 1, mid_p, new)
            new = jnp.where(lanes == hd + slots + 2, low_p, new)
            qa_ref[h, span, :] = new.astype(bf16)
        pair = jnp.where(lanes < hd, outs[0], pltpu.roll(outs[1], hd, 1))
        ctx_ref[g, half * BLK:(half + 1) * BLK, :] = pair.astype(bf16)
        if half == 0:
            ctx_ref[g, group:group + BLK, :] = outs[2].astype(bf16)
        else:
            both = jnp.where(lanes < hd, ctx_ref[g, group:group + BLK, :].astype(f32), pltpu.roll(outs[2], hd, 1))
            ctx_ref[g, group:group + BLK, :] = both.astype(bf16)

    def attend_group(g, _):
        attend(g, 0)
        attend(g, 1)
        return 0

    lax.fori_loop(0, rows // group, attend_group, 0)


def attend_back_kernel(heads, hd, len_ref, qa_ref, ka_ref, va_ref, kt_ref, ctx_ref, gctx_ref, lowt_ref,
                       g_ref, adp_ref, doa, dk, dv, dqt, dqs):
    rows = qa_ref.shape[1]
    slots = len_ref.shape[1]
    starts, ends = segment_bounds(len_ref, slots)
    dk[...] = jnp.zeros_like(dk)
    dv[...] = jnp.zeros_like(dv)
    lanes = lane_iota(BLK)
    left = lanes < hd
    group = ctx_ref.shape[1] * 2 // 3

    def back(g, half):
        row0 = pl.multiple_of(g * group + half * BLK, BLK)
        span = pl.ds(row0, BLK)
        lo, hi = block_range(starts, ends, row0)
        pair = gctx_ref[g, half * BLK:(half + 1) * BLK, :].astype(f32)
        last = gctx_ref[g, group:group + BLK, :].astype(f32)
        p_pair = pair * ctx_ref[g, half * BLK:(half + 1) * BLK, :].astype(f32)
        p_last = last * ctx_ref[g, group:group + BLK, :].astype(f32)
        deltas = [
            jnp.sum(jnp.where(left, p_pair, 0.0), axis=1, keepdims=True),
            jnp.sum(jnp.where(left, 0.0, p_pair), axis=1, keepdims=True),
            jnp.sum(jnp.where(left, p_last, 0.0) if half == 0 else jnp.where(left, 0.0, p_last), axis=1, keepdims=True),
        ]
        values = [pair, pltpu.roll(pair, hd, 1), last if half == 0 else pltpu.roll(last, hd, 1)]
        for h in range(heads):
            parts = three_parts(-jnp.broadcast_to(deltas[h], (BLK, LANES)))
            d = jnp.where(left, values[h], 0.0)
            for i, part in enumerate(parts):
                d = jnp.where(lanes == hd + i, part, d)
            doa[h] = d.astype(bf16)
        dqt[...] = jnp.zeros_like(dqt)

        def step(kb, _):
            keys = pl.ds(pl.multiple_of(kb * BLK, BLK), BLK)
            for h in range(heads):
                s = dot_nt(ka_ref[h, keys, :], qa_ref[h, span, :])
                p = jnp.exp2(s * LOG2E)
                dp = dot_nt(va_ref[h, keys, :], doa[h])
                ds = (p * dp).astype(bf16)
                dv[h, keys, :] += dot(p.astype(bf16), doa[h])
                dk[h, keys, :] += dot(ds, qa_ref[h, span, :])
                dqt[h * hd:(h + 1) * hd, :] += dot(kt_ref[h, :, keys], ds)
            return 0

        lax.fori_loop(lo, hi, step, 0)
        dqs[span, :] = (dqt[...].T * hd ** -0.5)

    def back_group(g, _):
        back(g, 0)
        back(g, 1)
        return 0

    lax.fori_loop(0, rows // group, back_group, 0)
    adp_ref[...] = jnp.zeros_like(adp_ref)

    def finish(i, _):
        span = pl.ds(pl.multiple_of(i * BLK, BLK), BLK)

        def pair(a, b):
            return jnp.where(left, a, pltpu.roll(b, hd, 1)).astype(bf16)

        g_ref[span, 0:LANES] = dqs[span, 0:LANES].astype(bf16)
        g_ref[span, LANES:2 * LANES] = pair(dqs[span, LANES:2 * LANES], dk[0, span, :])
        g_ref[span, 2 * LANES:3 * LANES] = pair(dk[1, span, :], dk[2, span, :])
        g_ref[span, 3 * LANES:4 * LANES] = pair(dv[0, span, :], dv[1, span, :])
        g_ref[span, 4 * LANES:5 * LANES] = pair(dv[2, span, :], jnp.zeros((BLK, LANES), f32))
        adp_ref[...] += 2.0 * dot(lowt_ref[:, span], g_ref[span, :])
        return 0

    lax.fori_loop(0, rows // BLK, finish, 0)


def phi_parts(a):
    z = jnp.abs(a)
    t = 1.0 / (1.0 + 0.23164188 * z)
    e = jnp.exp2(a * a * (-0.5 * LOG2E))
    q = t * (0.127414796 + t * (-0.142248368 + t * (0.710706871 + t * (-0.726576014 + t * 0.530702714))))
    tail = q * e
    return jnp.where(a >= 0.0, 1.0 - tail, tail), e


def peers(t):
    return (t, t + 1 - 2 * lax.rem(t, 2), lax.rem(t + 2, 4), 3 - t)


def middle_kernel(hd, len_ref, ctx_ref, tok_ref, cot_ref, ow_ref, owy_ref, fi_ref, fiy_ref, fo_ref, foy_ref,
                  g1_ref, g2_ref, act_ref, gmix_ref, gctx_ref,
                  xin, xb, wout, wfi, wfo, tokr, cotr, normed, unit1, inv1, low, acc, gel, gsend, grecv,
                  wsem_s, wsem_r, lsem, csem_s, csem_r, gsem_s, gsem_r):
    me = lax.axis_index("tensor")
    ids = peers(me)
    own = tokr.shape[0]
    feat = tokr.shape[1]
    part = ow_ref.shape[0]
    half = own // 2

    def there(s):
        return {"tensor": ids[s]}

    barrier = pltpu.get_barrier_semaphore()
    for s in (1, 2, 3):
        pl.semaphore_signal(barrier, inc=1, device_id=there(s), device_id_type=pl.DeviceIdType.MESH)
    pl.semaphore_wait(barrier, 3)

    ctx_copies = []
    for s in (2, 3, 1):
        ctx_copies.append([
            pltpu.make_async_remote_copy(
                src_ref=ctx_ref.at[ids[s]], dst_ref=xb.at[s], send_sem=csem_s.at[s], recv_sem=csem_r.at[s],
                device_id=there(s), device_id_type=pl.DeviceIdType.MESH), s])
        ctx_copies[-1][0].start()
    ctx_own = pltpu.make_async_copy(ctx_ref.at[me], xb.at[0], lsem.at[0])
    ctx_own.start()
    rows = pl.ds(pl.multiple_of(me * own, own), own)
    tok_copy = pltpu.make_async_copy(tok_ref.at[rows], tokr, lsem.at[1])
    tok_copy.start()
    cot_copy = pltpu.make_async_copy(cot_ref.at[rows], cotr, lsem.at[2])
    cot_copy.start()
    local, remote = [], []
    for i, (src, srcy, dst) in enumerate(((ow_ref, owy_ref, wout), (fi_ref, fiy_ref, wfi), (fo_ref, foy_ref, wfo))):
        for j, (ref, mine, theirs) in enumerate(((src, 0, 1), (srcy, 2, 3))):
            n = 2 * i + j
            if i == 0:
                to_mine, to_theirs = dst.at[mine, 0:part], dst.at[theirs, 0:part]
            else:
                to_mine, to_theirs = dst.at[mine], dst.at[theirs]
            c = pltpu.make_async_copy(ref, to_mine, lsem.at[3 + n])
            r = pltpu.make_async_remote_copy(
                src_ref=ref, dst_ref=to_theirs, send_sem=wsem_s.at[n], recv_sem=wsem_r.at[n],
                device_id=there(1), device_id_type=pl.DeviceIdType.MESH)
            c.start()
            r.start()
            local.append(c)
            remote.append(r)
    padrows = wout.shape[1] - part
    for s in range(4):
        wout[s, part:, :] = jnp.zeros((padrows, feat), bf16)

    for n in (0, 1):
        local[n].wait()
        remote[n].wait_recv()
    ctx_own.wait()
    tok_copy.wait()
    cot_copy.wait()
    for c, s in ctx_copies:
        c.wait_recv()

    lanes = lane_iota(half)
    for s in range(4):
        xin[:, s * 2 * LANES:s * 2 * LANES + LANES] = xb[s, 0:own, :]
        b = xb[s, own:, :]
        xin[0:half, s * 2 * LANES + LANES:(s + 1) * 2 * LANES] = b
        xin[half:, s * 2 * LANES + LANES:(s + 1) * 2 * LANES] = pltpu.roll(b.astype(f32), hd, 1).astype(bf16)

    wflat = wout.reshape(4 * 2 * LANES, feat)
    acc[...] = dot(xin[...], wflat[...])
    CH = 64
    n_valid = jnp.int32(0)
    for s in range(len_ref.shape[1] - 1):
        n_valid = n_valid + len_ref[0, s]
    g1 = g1_ref[...]
    g2 = g2_ref[...]

    def norm_one(i, _):
        sp = pl.ds(pl.multiple_of(i * CH, CH), CH)
        v = tokr[sp, :].astype(f32) + acc[sp, :]
        mean = jnp.mean(v, axis=-1, keepdims=True)
        c = v - mean
        inv = lax.rsqrt(jnp.mean(c * c, axis=-1, keepdims=True) + EPSILON)
        u = c * inv
        unit1[sp, :] = u
        inv1[sp, :] = jnp.broadcast_to(inv, (CH, LANES))
        nrm = u * g1
        normed[sp, :] = nrm
        low[sp, :] = nrm.astype(bf16)
        return 0

    lax.fori_loop(0, own // CH, norm_one, 0)

    for s in (0, 2, 1, 3):
        n_in, n_out = {0: (2, 4), 2: (3, 5), 1: (2, 4), 3: (3, 5)}[s]
        if s in (0, 2):
            local[n_in].wait()
            local[n_out].wait()
        else:
            remote[n_in].wait_recv()
            remote[n_out].wait_recv()

        for r in range(0, own, BLK):
            pre = dot(low[r:r + BLK, :], wfi[s])
            cdf, e = phi_parts(pre)
            gel[s, r:r + BLK, :] = (cdf + pre * e * 0.3989422804014327).astype(bf16)
            out = dot((pre * cdf).astype(bf16), wfo[s])
            if s == 0:
                acc[r:r + BLK, :] = out
            else:
                acc[r:r + BLK, :] += out

    def norm_two(i, _):
        sp = pl.ds(pl.multiple_of(i * CH, CH), CH)
        v = normed[sp, :] + acc[sp, :]
        mean = jnp.mean(v, axis=-1, keepdims=True)
        c = v - mean
        inv = lax.rsqrt(jnp.mean(c * c, axis=-1, keepdims=True) + EPSILON)
        u = c * inv
        pos = me * own + i * CH + lax.broadcasted_iota(jnp.int32, (CH, 1), 0)
        valid = jnp.where(pos < n_valid, 1.0, 0.0)
        act_ref[sp, :] = (u * g2 * valid).astype(bf16)
        w = cotr[sp, :].astype(f32) * valid * g2
        gm = inv * (w - jnp.mean(w, axis=-1, keepdims=True) - u * jnp.mean(w * u, axis=-1, keepdims=True))
        acc[sp, :] = gm
        low[sp, :] = gm.astype(bf16)
        return 0

    lax.fori_loop(0, own // CH, norm_two, 0)

    for s in range(4):
        for r in range(0, own, BLK):
            ga = dot_nt(low[r:r + BLK, :], wfo[s])
            gp = (ga * gel[s, r:r + BLK, :].astype(f32)).astype(bf16)
            acc[r:r + BLK, :] += dot_nt(gp, wfi[s])

    def norm_back(i, _):
        sp = pl.ds(pl.multiple_of(i * CH, CH), CH)
        w = acc[sp, :] * g1
        u = unit1[sp, :]
        inv = inv1[sp, 0:1]
        gm = inv * (w - jnp.mean(w, axis=-1, keepdims=True) - u * jnp.mean(w * u, axis=-1, keepdims=True))
        gmix_ref[sp, :] = gm
        low[sp, :] = gm.astype(bf16)
        return 0

    lax.fori_loop(0, own // CH, norm_back, 0)

    sends = []
    for s in (2, 3, 1, 0):
        g = dot_nt(low[...], wout[s])
        gsend[s, 0:own, :] = g[:, 0:LANES].astype(bf16)
        b = jnp.where(lanes < hd, g[0:half, LANES:], pltpu.roll(g[half:, LANES:], hd, 1))
        gsend[s, own:, :] = b.astype(bf16)
        if s:
            c = pltpu.make_async_remote_copy(
                src_ref=gsend.at[s], dst_ref=grecv.at[s], send_sem=gsem_s.at[s], recv_sem=gsem_r.at[s],
                device_id=there(s), device_id_type=pl.DeviceIdType.MESH)
            c.start()
            sends.append((c, s))
    outs = [pltpu.make_async_copy(gsend.at[0], gctx_ref.at[me], lsem.at[0])]
    outs[0].start()
    for c, s in sends[::-1]:
        c.wait_recv()
        o = pltpu.make_async_copy(grecv.at[s], gctx_ref.at[ids[s]], lsem.at[s])
        o.start()
        outs.append(o)
    for c, s in sends:
        c.wait_send()
    for c, s in ctx_copies:
        c.wait_send()
    for c in remote:
        c.wait_send()
    for o in outs:
        o.wait()


def last_kernel(n_dp, g_ref, weff_ref, gmix_ref, adp_ref, out_ref, sum_ref,
                gs, wp, psend, precv, asend, arecv,
                ssem, rsem, lsem, psem_s, psem_r, asem_s, asem_r):
    me = lax.axis_index("tensor")
    dp = lax.axis_index("dp")
    ids = peers(me)
    own = out_ref.shape[0]

    def there(s):
        return {"tensor": ids[s]}

    def row(d):
        return {"dp": lax.rem(dp + d, n_dp)}

    barrier = pltpu.get_barrier_semaphore()
    for s in (1, 2):
        pl.semaphore_signal(barrier, inc=1, device_id=there(s), device_id_type=pl.DeviceIdType.MESH)
    for d in range(1, n_dp):
        pl.semaphore_signal(barrier, inc=1, device_id=row(d), device_id_type=pl.DeviceIdType.MESH)
    pl.semaphore_wait(barrier, 2 + n_dp - 1)

    def group(s):
        return g_ref.at[pl.ds(pl.multiple_of(ids[s] * own, own), own)]

    def remote(src, dst, i):
        c = pltpu.make_async_remote_copy(src_ref=src, dst_ref=dst, send_sem=ssem.at[i], recv_sem=rsem.at[i],
                                         device_id=there(1), device_id_type=pl.DeviceIdType.MESH)
        c.start()
        return c

    sent = [remote(group(3), gs.at[0, 1], 0), remote(weff_ref, wp.at[1], 1), remote(group(1), gs.at[1, 1], 2)]
    local = [pltpu.make_async_copy(group(2), gs.at[0, 0], lsem.at[0]),
             pltpu.make_async_copy(weff_ref, wp.at[0], lsem.at[1]),
             pltpu.make_async_copy(group(0), gs.at[1, 0], lsem.at[2])]
    for c in local:
        c.start()
    half = adp_ref.shape[0] // 2
    wide = 2 * LANES
    cols = adp_ref.shape[1]
    asend[:, 0:wide] = adp_ref[0:half, 0:wide]
    asend[:, wide:] = adp_ref[half:, cols - wide:]
    asent = []
    for d in range(1, n_dp):
        c = pltpu.make_async_remote_copy(src_ref=asend, dst_ref=arecv.at[d], send_sem=asem_s.at[d], recv_sem=asem_r.at[d],
                                         device_id=row(d), device_id_type=pl.DeviceIdType.MESH)
        c.start()
        asent.append(c)
    local[0].wait()
    local[1].wait()
    sent[0].wait_recv()
    sent[1].wait_recv()
    psent = []
    for i in range(own // LANES):
        sp = slice(i * LANES, (i + 1) * LANES)
        psend[sp, :] = (dot_nt(gs[0, 0, sp, :], wp[0]) + dot_nt(gs[0, 1, sp, :], wp[1])).astype(bf16)
        c = pltpu.make_async_remote_copy(src_ref=psend.at[sp], dst_ref=precv.at[sp], send_sem=psem_s.at[i],
                                         recv_sem=psem_r.at[i], device_id=there(2), device_id_type=pl.DeviceIdType.MESH)
        c.start()
        psent.append(c)
    local[2].wait()
    sent[2].wait_recv()
    for i in range(own // LANES):
        sp = slice(i * LANES, (i + 1) * LANES)
        out_ref[sp, :] = gmix_ref[sp, :] + (dot_nt(gs[1, 0, sp, :], wp[0]) + dot_nt(gs[1, 1, sp, :], wp[1]))
    total = asend[...]
    for c in asent:
        c.wait_recv()
    for d in range(1, n_dp):
        total = total + arecv[d]
    sum_ref[...] = total
    for i in range(own // LANES):
        sp = slice(i * LANES, (i + 1) * LANES)
        psent[i].wait_recv()
        out_ref[sp, :] += precv[sp, :].astype(f32)
    for c in psent + sent + asent:
        c.wait_send()


def vmem(shape, dtype):
    return pltpu.VMEM(shape, dtype)


V = pl.BlockSpec(memory_space=pltpu.VMEM)
S = pl.BlockSpec(memory_space=pltpu.SMEM)
ANY = pl.BlockSpec(memory_space=pl.ANY)


def on_device(n_dp, groups, tokens, seq_lengths, query_weight, key_weight, value_weight, out_weight, ffn_in, ffn_out,
              gain_attn, gain_ffn, query_down, value_down, query_up, value_up, cotangent):
    rows, feat = tokens.shape
    width = query_weight.shape[1]
    rank, heads, hd = query_up.shape
    hidden = ffn_in.shape[1]
    own = rows // groups
    packed = own + own // 2
    pack = 5 * LANES
    shape = jax.ShapeDtypeStruct
    y_pairs = [(i, i ^ 2) for i in range(groups)]
    out_y = lax.ppermute(out_weight, "tensor", y_pairs)
    fi_y = lax.ppermute(ffn_in, "tensor", y_pairs)
    fo_y = lax.ppermute(ffn_out, "tensor", y_pairs)

    dma = pltpu.SemaphoreType.DMA
    qa, ka, va, kt, ctx, lowt, weff = pl.pallas_call(
        functools.partial(attend_kernel, heads, hd),
        out_shape=(shape((heads, rows, LANES), bf16), shape((heads, rows, LANES), bf16), shape((heads, rows, LANES), bf16),
                   shape((heads, hd, rows), bf16), shape((groups, packed, LANES), bf16), shape((2 * rank, rows), bf16),
                   shape((feat, pack), bf16)),
        in_specs=[S] + [V] * 8,
        out_specs=(V,) * 7,
        scratch_shapes=[vmem((feat, 3 * heads * LANES + LANES), bf16), vmem((LANES, 2 * heads * LANES), bf16),
                        vmem((heads, 5, BLK, BLK), f32), vmem((heads, BLK, LANES), f32), vmem((heads, BLK, LANES), f32)],
        compiler_params=pltpu.CompilerParams(vmem_limit_bytes=VMEM_LIMIT),
        cost_estimate=pl.CostEstimate(flops=20 * 10**9, bytes_accessed=20 * 2**20, transcendentals=4 * 10**6),
        name="attend",
    )(seq_lengths, tokens, query_weight, key_weight, value_weight, query_down, value_down,
      query_up.reshape(rank, width), value_up.reshape(rank, width))

    act, gmix, gctx = pl.pallas_call(
        functools.partial(middle_kernel, hd),
        out_shape=(shape((own, feat), bf16), shape((own, feat), f32), shape((groups, packed, LANES), bf16)),
        in_specs=[S] + [ANY] * 9 + [V] * 2,
        out_specs=(V, V, ANY),
        scratch_shapes=[
            vmem((own, groups * 2 * LANES), bf16), vmem((groups, packed, LANES), bf16), vmem((groups, 2 * LANES, feat), bf16),
            vmem((groups, feat, hidden), bf16), vmem((groups, hidden, feat), bf16), vmem((own, feat), bf16), vmem((own, feat), bf16),
            vmem((own, feat), f32), vmem((own, feat), f32), vmem((own, LANES), f32), vmem((own, feat), bf16), vmem((own, feat), f32),
            vmem((groups, own, hidden), bf16), vmem((groups, packed, LANES), bf16), vmem((groups, packed, LANES), bf16),
            dma((6,)), dma((6,)), dma((9,)), dma((4,)), dma((4,)), dma((4,)), dma((4,))],
        compiler_params=pltpu.CompilerParams(vmem_limit_bytes=VMEM_LIMIT, collective_id=0, has_side_effects=True),
        cost_estimate=pl.CostEstimate(flops=11 * 10**9, bytes_accessed=20 * 2**20, transcendentals=4 * 10**6),
        name="middle",
    )(seq_lengths, ctx, tokens, cotangent, out_weight, out_y, ffn_in, fi_y, ffn_out, fo_y,
      gain_attn.reshape(1, feat), gain_ffn.reshape(1, feat))

    grads, adapter = pl.pallas_call(
        functools.partial(attend_back_kernel, heads, hd),
        out_shape=(shape((rows, pack), bf16), shape((2 * rank, pack), f32)),
        in_specs=[S] + [V] * 7,
        out_specs=(V, V),
        scratch_shapes=[vmem((heads, BLK, LANES), bf16), vmem((heads, rows, LANES), f32), vmem((heads, rows, LANES), f32),
                        vmem((2 * LANES, BLK), f32), vmem((rows, 2 * LANES), f32)],
        compiler_params=pltpu.CompilerParams(vmem_limit_bytes=VMEM_LIMIT),
        cost_estimate=pl.CostEstimate(flops=20 * 10**9, bytes_accessed=20 * 2**20, transcendentals=4 * 10**6),
        name="attend_back",
    )(seq_lengths, qa, ka, va, kt, ctx, gctx, lowt)

    grad_input, adapter_sum = pl.pallas_call(
        functools.partial(last_kernel, n_dp),
        out_shape=(shape((own, feat), f32), shape((rank, 4 * LANES), f32)),
        in_specs=[ANY, ANY, V, V],
        out_specs=(V, V),
        scratch_shapes=[
            vmem((2, 2, own, pack), bf16), vmem((2, feat, pack), bf16), vmem((own, feat), bf16), vmem((own, feat), bf16),
            vmem((rank, 4 * LANES), f32), vmem((n_dp, rank, 4 * LANES), f32),
            dma((3,)), dma((3,)), dma((3,)), dma((4,)), dma((4,)), dma((n_dp,)), dma((n_dp,))],
        compiler_params=pltpu.CompilerParams(vmem_limit_bytes=VMEM_LIMIT, collective_id=1, has_side_effects=True),
        cost_estimate=pl.CostEstimate(flops=2 * 10**9, bytes_accessed=10 * 2**20, transcendentals=0),
        name="last",
    )(grads, weff, gmix, adapter)

    cols = hd // n_dp
    first = lax.axis_index("dp") * cols

    def pick(x):
        return lax.dynamic_slice_in_dim(x.reshape(rank, heads, hd), first, cols, 2)

    up_q = pick(adapter_sum[:, 0:width])
    up_v = pick(adapter_sum[:, 4 * LANES - width - hd:4 * LANES - hd])
    return act, grad_input, up_q, up_v


def solution(mesh):
    in_specs = (
        P("dp", None), P("dp", None), P(None, "tensor"), P(None, "tensor"), P(None, "tensor"), P("tensor", None),
        P(None, "tensor"), P("tensor", None), P(), P(), P(), P(), P(None, "tensor", None), P(None, "tensor", None),
        P("dp", None),
    )
    out_specs = (P(("dp", "tensor"), None), P(("dp", "tensor"), None), P(None, "tensor", "dp"), P(None, "tensor", "dp"))
    return jax.shard_map(
        functools.partial(on_device, mesh.shape["dp"], mesh.shape["tensor"]),
        mesh=mesh, in_specs=in_specs, out_specs=out_specs, check_vma=False,
    )
```

```python
import functools

import jax
import jax.numpy as jnp
from jax import lax
from jax.experimental import pallas as pl
from jax.experimental.pallas import tpu as pltpu
from jax.sharding import PartitionSpec as P

EPSILON = 1e-05
BLOCKED = -1e30
LOG2E = 1.4426950408889634
BLK = 256
HALF = BLK // 2
LANES = 128
REACH = 2
f32 = jnp.float32
bf16 = jnp.bfloat16
VMEM_LIMIT = 64 * 1024 * 1024 - 65536
MESH = pl.DeviceIdType.MESH
TN = (((0,), (0,)), ((), ()))


def dot(a, b):
    return jnp.dot(a, b, preferred_element_type=f32)


def dot_nt(a, b):
    return lax.dot_general(a, b, (((1,), (1,)), ((), ())), preferred_element_type=f32)


def iota(shape, axis):
    return lax.broadcasted_iota(jnp.int32, shape, axis)


def three_parts(x):
    hi = x.astype(bf16).astype(f32)
    mid = (x - hi).astype(bf16).astype(f32)
    low = (x - hi - mid).astype(bf16).astype(f32)
    return hi, mid, low


def phi_parts(a):
    z = jnp.abs(a)
    t = 1.0 / (1.0 + 0.23164188 * z)
    e = jnp.exp2(a * a * (-0.5 * LOG2E))
    q = t * (0.127414796 + t * (-0.142248368 + t * (0.710706871 + t * (-0.726576014 + t * 0.530702714))))
    tail = q * e
    return jnp.where(a >= 0.0, 1.0 - tail, tail), e


def moments(v):
    mean = jnp.mean(v, axis=-1, keepdims=True)
    c = v - mean
    inv = lax.rsqrt(jnp.mean(c * c, axis=-1, keepdims=True) + EPSILON)
    return c * inv, inv


def pull(w, u, inv):
    return inv * (w - jnp.mean(w, axis=-1, keepdims=True) - u * jnp.mean(w * u, axis=-1, keepdims=True))


class Bag:
    pass


def layer_kernel(n_dp, heads, hd, names, *refs):
    z = Bag()
    for name, ref in zip(names, refs):
        setattr(z, name, ref)
    rows, feat = z.tok.shape
    blocks = rows // BLK
    own = z.out.shape[0]
    per = own // BLK
    width = heads * hd
    slots = z.lens.shape[1]
    rank = z.dq.shape[0]
    pack = z.weff.shape[0]
    part = z.ow.shape[0]
    me = lax.axis_index("tensor")
    dp = lax.axis_index("dp")
    yy, cc = lax.div(me, 2), lax.rem(me, 2)
    px, pz = lax.rem(dp, 2), lax.rem(lax.div(dp, 2), 2)

    def member(k):
        fy = 1 - k // 2
        fc = (k % 2 + k // 2) % 2
        return 2 * lax.rem(yy + fy, 2) + lax.rem(cc + fc, 2)

    def tensor_at(k):
        return {"tensor": member(k)}

    x_peer = {"dp": dp + 1 - 2 * px}
    z_peer = {"dp": dp + 2 - 4 * pz}

    def row_at(d):
        return {"dp": lax.rem(dp + d, n_dp)}

    def remote(src, dst, send, recv, device):
        return pltpu.make_async_remote_copy(src_ref=src, dst_ref=dst, send_sem=send, recv_sem=recv,
                                            device_id=device, device_id_type=MESH)

    per_chunk = rows // 4
    tok_in = [pltpu.make_async_copy(z.tok_hbm.at[pl.ds(j * per_chunk, per_chunk)], z.tok.at[pl.ds(j * per_chunk, per_chunk)],
                                    z.lsem.at[j]) for j in range(4)]
    cot_in = pltpu.make_async_copy(z.cot_hbm.at[pl.ds(pl.multiple_of(me * own, own), own)], z.cot, z.lsem.at[4])
    weights = ((z.ow, z.wout), (z.fi, z.wfi), (z.fo, z.wfo))

    def full(dst, k):
        return dst.at[k, 0:part] if dst is z.wout else dst.at[k]

    own_w = [pltpu.make_async_copy(src, full(dst, 3), z.lsem.at[5 + i]) for i, (src, dst) in enumerate(weights)]
    for c in tok_in + own_w + [cot_in]:
        c.start()
    barrier = pltpu.get_barrier_semaphore()
    for k in range(3):
        pl.semaphore_signal(barrier, inc=1, device_id=tensor_at(k), device_id_type=MESH)
    for d in range(1, n_dp):
        pl.semaphore_signal(barrier, inc=1, device_id=row_at(d), device_id_type=MESH)

    z.weff[width:2 * width, :] = z.wk[...]
    for base, w_ref, d_ref, u_ref in ((0, z.wq, z.dq, z.uq), (2 * width, z.wv, z.dv, z.uv)):
        for h in range(heads):
            low_rank = lax.dot_general(u_ref[h], d_ref[...], TN, preferred_element_type=f32)
            mine = w_ref[h * hd:(h + 1) * hd, :].astype(f32) + 2.0 * low_rank
            z.weff[base + h * hd:base + (h + 1) * hd, :] = mine.astype(bf16)
    downs = jnp.concatenate([z.dq[...].astype(f32), z.dv[...].astype(f32)], axis=0)
    z.weff[3 * width:3 * width + 2 * rank, :] = downs.astype(bf16)
    z.weff[3 * width + 2 * rank:, :] = jnp.zeros((pack - 3 * width - 2 * rank, feat), bf16)
    for h in range(heads):
        z.vt[h, hd:, :] = jnp.ones((z.vt.shape[1] - hd, rows), bf16)
    for k in range(4):
        z.wout[k, part:, :] = jnp.zeros((z.wout.shape[1] - part, feat), bf16)
    pl.semaphore_wait(barrier, 3 + n_dp - 1)

    def quarter(dst, k, dx, dz):
        n = (part if dst is z.wout else dst.shape[1]) // 4
        q = 2 * lax.rem(pz + dz, 2) + lax.rem(px + dx, 2)
        return dst.at[k, pl.ds(pl.multiple_of(q * n, n), n)]

    def quarter_of(src):
        n = src.shape[0] // 4
        return src.at[pl.ds(pl.multiple_of((2 * pz + px) * n, n), n)]

    moves = []
    for i, (src, dst) in enumerate(weights):
        v = Bag()
        x_first = i < 2
        sem = lambda j, i=i: (z.wsem_s.at[i, j], z.wsem_r.at[i, j])
        v.a = remote(quarter_of(src), quarter(dst, 0, 0, 0), *sem(0), tensor_at(0))
        v.partner = remote(src, full(dst, 2), *sem(1), tensor_at(2))
        v.x = remote(quarter(dst, 0, 0, 0), quarter(dst, 0, 0, 0), *sem(2), x_peer)
        v.z = remote(quarter(dst, 0, 0, 0), quarter(dst, 0, 0, 0), *sem(3), z_peer)
        far = (1, 0) if x_first else (0, 1)
        v.second = remote(quarter(dst, 0, *far), quarter(dst, 0, *far), *sem(4), z_peer if x_first else x_peer)
        v.first, v.other = (v.x, v.z) if x_first else (v.z, v.x)
        v.d = [remote(quarter(dst, 0, *q), quarter(dst, 1, *q), *sem(5 + j), tensor_at(2))
               for j, q in enumerate(((0, 0), far, far[::-1], (1, 1)))]
        moves.append(v)
    for v in moves:
        v.a.start()
    weff_out = remote(z.weff, z.weffp, z.esem_s.at[0], z.esem_r.at[0], tensor_at(2))
    for v in moves:
        v.partner.start()
    weff_out.start()

    def relay1(i):
        moves[i].a.wait_recv()
        moves[i].first.start()
        moves[i].other.start()
        moves[i].d[0].start()

    def relay2(i):
        moves[i].first.wait_recv()
        moves[i].second.start()
        moves[i].d[1].start()

    def relay3(i):
        moves[i].other.wait_recv()
        moves[i].d[2].start()

    def relay4(i):
        moves[i].second.wait_recv()
        moves[i].d[3].start()

    def arrive(i):
        for c in moves[i].d:
            c.wait_recv()

    starts, ends = [], []
    total = jnp.int32(0)
    for s in range(slots):
        starts.append(total)
        total = total + z.lens[0, s]
        ends.append(total)
    n_valid = ends[slots - 2]
    lane = iota((1, LANES), 1)
    seg_start = jnp.zeros((1, LANES), jnp.int32)
    seg_end = jnp.zeros((1, LANES), jnp.int32)
    for s in range(slots):
        seg_start = jnp.where(lane == hd + s, starts[s], seg_start)
        seg_end = jnp.where(lane == hd + s, ends[s], seg_end)
    is_mask = (lane >= hd) & (lane < hd + slots)
    extra = jnp.where((lane >= hd + slots) & (lane < hd + slots + 3), 1.0, 0.0)
    ones_v = jnp.where((lane >= hd) & (lane < hd + 3), 1.0, 0.0)
    lanes = iota((BLK, LANES), 1)
    left = lanes < hd

    def span_of(b):
        return pl.ds(pl.multiple_of(b * BLK, BLK), BLK)

    def project(i, _):
        for j in range(4):
            @pl.when(i == j * (blocks // 4))
            def _():
                tok_in[j].wait()
        span = span_of(i)
        y = dot_nt(z.tok[span, :], z.weff[...])
        pos = i * BLK + iota((BLK, LANES), 0)
        mine = (pos >= seg_start) & (pos < seg_end)
        q_mask = jnp.where(mine, 1.0, 0.0)
        k_mask = jnp.where(is_mask & jnp.logical_not(mine), BLOCKED, extra)
        for c in range(pack // LANES):
            z.yt[c * LANES:(c + 1) * LANES, span] = y[:, c * LANES:(c + 1) * LANES].T.astype(bf16)

        def head(n):
            tile = y[:, (n // 2) * LANES:(n // 2 + 1) * LANES]
            return tile if n % 2 == 0 else pltpu.roll(tile, hd, 1)

        for h in range(heads):
            z.qa[h, span, :] = jnp.where(left, head(h) * hd ** -0.5, q_mask).astype(bf16)
            z.ka[h, span, :] = jnp.where(left, head(heads + h), k_mask).astype(bf16)
            z.va[h, span, :] = jnp.where(left, head(2 * heads + h), ones_v).astype(bf16)
            n = (2 * heads + h) * hd
            z.vt[h, 0:hd, span] = z.yt[n:n + hd, span]
        return 0

    lax.fori_loop(0, blocks, project, 0)
    relay1(0)

    def block_of(g, h):
        return per * g + h + lax.div(g, 2) * (1 - 2 * h)

    def key_range(qb):
        return jnp.maximum(qb - REACH, 0), jnp.minimum(qb + REACH + 1, blocks)

    def ctx_copy(k, h):
        return remote(z.xsend.at[k, h], z.xb.at[k, h], z.csem_s.at[k, h], z.csem_r.at[k, h], tensor_at(k))

    sub = iota((hd, BLK), 0)
    depth = z.vt.shape[1]

    def attend(n, _):
        h2, k2 = lax.div(n, 4), lax.rem(n, 4)
        fy = 1 - lax.div(k2, 2)
        fc = lax.rem(lax.rem(k2, 2) + lax.div(k2, 2), 2)
        g = 2 * lax.rem(yy + fy, 2) + lax.rem(cc + fc, 2)
        qb = block_of(g, h2)
        span = span_of(qb)
        lo, hi = key_range(qb)
        z.oacc[...] = jnp.zeros_like(z.oacc)
        z.peak[...] = jnp.full(z.peak.shape, BLOCKED, f32)

        def score(h, kb):
            z.sbuf[h] = dot_nt(z.ka[h, span_of(kb), :], z.qa[h, span, :])

        for h in range(heads):
            score(h, lo)

        def keys(kb, _):
            later = jnp.minimum(kb + 1, hi - 1)
            for h in range(heads):
                s = z.sbuf[h]
                old = z.peak[h:h + 1, :]
                new = jnp.maximum(old, jnp.max(s, axis=0, keepdims=True))
                p = jnp.exp2((s - new) * LOG2E).astype(bf16)
                z.peak[h:h + 1, :] = new
                scale = jnp.exp2((old - new) * LOG2E)
                z.oacc[h] = z.oacc[h] * scale + dot(z.vt[h, :, span_of(kb)], p)
                score(h, later)
            return 0

        lax.fori_loop(lo, hi, keys, 0)
        outs = []
        for h in range(heads):
            weight = z.oacc[h, hd:hd + 1, :]
            o = z.oacc[h, 0:hd, :] * (1.0 / weight)
            z.ot[h * hd:(h + 1) * hd, span] = o.astype(bf16)
            parts = three_parts(-(z.peak[h:h + 1, :] + jnp.log(weight)))
            tail = jnp.zeros((hd, BLK), f32)
            for j, p in enumerate(parts):
                tail = jnp.where(sub == slots + j, p, tail)
            t = jnp.concatenate([o, tail], axis=0).T
            outs.append(t)
            in_tail = (lanes >= hd + slots) & (lanes < hd + slots + 3)
            z.qa[h, span, :] = jnp.where(in_tail, t, z.qa[h, span, :].astype(f32)).astype(bf16)
        z.xsend[k2, h2, 0:BLK, :] = jnp.where(left, outs[0], pltpu.roll(outs[1], hd, 1)).astype(bf16)
        z.xsend[k2, h2, BLK:, :] = jnp.where(left[0:HALF], outs[2][0:HALF], pltpu.roll(outs[2][HALF:], hd, 1)).astype(bf16)

        @pl.when(k2 < 3)
        def _():
            remote(z.xsend.at[k2, h2], z.xb.at[k2, h2], z.csem_s.at[k2, h2], z.csem_r.at[k2, h2], {"tensor": g}).start()

        @pl.when(n == 2)
        def _():
            relay2(0)

        @pl.when(n == 3)
        def _():
            relay1(1)

        @pl.when(n == 4)
        def _():
            relay3(0)
            relay4(0)

        return 0

    lax.fori_loop(0, 2 * 4, attend, 0)

    wflat = z.wout.reshape(4 * 2 * LANES, feat)
    g1 = z.g1[...]
    g2 = z.g2[...]
    CH = 64

    def my_rows(h):
        return (h + yy * (1 - 2 * h)) * BLK

    def front(h, _):
        hs = span_of(h)

        @pl.when(h == 0)
        def _():
            own_w[0].wait()
            moves[0].partner.wait_recv()
            arrive(0)

        for k in range(3):
            ctx_copy(k, h).wait_recv()
        for k in range(4):
            src = z.xsend if k == 3 else z.xb
            z.xin[:, 2 * k * LANES:(2 * k + 1) * LANES] = src[k, h, 0:BLK, :]
            b = src[k, h, BLK:, :]
            z.xin[0:HALF, (2 * k + 1) * LANES:(2 * k + 2) * LANES] = b
            z.xin[HALF:, (2 * k + 1) * LANES:(2 * k + 2) * LANES] = pltpu.roll(b.astype(f32), hd, 1).astype(bf16)
        z.acc[hs, :] = dot(z.xin[...], wflat[...])
        row0 = me * own + my_rows(h)

        def norm_one(i, _):
            sp = pl.ds(pl.multiple_of(h * BLK + i * CH, CH), CH)
            tp = pl.ds(pl.multiple_of(row0 + i * CH, CH), CH)
            u, inv = moments(z.tok[tp, :].astype(f32) + z.acc[sp, :])
            z.unit1[sp, :] = u
            z.inv1[sp, :] = jnp.broadcast_to(inv, (CH, LANES))
            z.normed[sp, :] = u * g1
            z.low[sp, :] = (u * g1).astype(bf16)
            return 0

        lax.fori_loop(0, BLK // CH, norm_one, 0)

        @pl.when(h == 0)
        def _():
            relay2(1)
            own_w[1].wait()
            own_w[2].wait()
            moves[1].partner.wait_recv()
            moves[2].partner.wait_recv()

        pre = dot(z.low[hs, :], z.wfi[3])
        for k in (3, 2):
            later = dot(z.low[hs, :], z.wfi[2]) if k == 3 else None
            cdf, e = phi_parts(pre)
            z.gel[k, hs, :] = (cdf + pre * e * 0.3989422804014327).astype(bf16)
            out = dot((pre * cdf).astype(bf16), z.wfo[k])
            z.acc[hs, :] = out if k == 3 else z.acc[hs, :] + out
            pre = later

        @pl.when(h == 0)
        def _():
            relay3(1)
            relay1(2)

        return 0

    lax.fori_loop(0, 2, front, 0)
    relay4(1)
    cot_in.wait()

    def grad_copy(k, h):
        return remote(z.gsend.at[k, h], z.grecv.at[me, h], z.gsem_s.at[k, h], z.gsem_r.at[k, h], tensor_at(k))

    def rear(h, _):
        hs = span_of(h)

        @pl.when(h == 0)
        def _():
            arrive(1)

        pre = dot(z.low[hs, :], z.wfi[0])
        for k in range(2):
            later = dot(z.low[hs, :], z.wfi[1]) if k == 0 else None
            cdf, e = phi_parts(pre)
            z.gel[k, hs, :] = (cdf + pre * e * 0.3989422804014327).astype(bf16)
            z.actv[k] = (pre * cdf).astype(bf16)
            pre = later

        @pl.when(h == 0)
        def _():
            relay2(2)
            relay3(2)
            relay4(2)
            arrive(2)

        z.acc[hs, :] += dot(z.actv[0], z.wfo[0]) + dot(z.actv[1], z.wfo[1])
        row0 = my_rows(h)

        def norm_two(i, _):
            sp = pl.ds(pl.multiple_of(h * BLK + i * CH, CH), CH)
            tp = pl.ds(pl.multiple_of(row0 + i * CH, CH), CH)
            u, inv = moments(z.normed[sp, :] + z.acc[sp, :])
            pos = me * own + row0 + i * CH + iota((CH, 1), 0)
            valid = jnp.where(pos < n_valid, 1.0, 0.0)
            z.act[tp, :] = (u * g2 * valid).astype(bf16)
            gm = pull(z.cot[tp, :].astype(f32) * valid * g2, u, inv)
            z.acc[sp, :] = gm
            z.low[sp, :] = gm.astype(bf16)
            return 0

        lax.fori_loop(0, BLK // CH, norm_two, 0)
        ga = dot_nt(z.low[hs, :], z.wfo[0])
        for k in range(4):
            later = dot_nt(z.low[hs, :], z.wfo[k + 1]) if k < 3 else None
            z.acc[hs, :] += dot_nt((ga * z.gel[k, hs, :].astype(f32)).astype(bf16), z.wfi[k])
            ga = later

        def norm_back(i, _):
            sp = pl.ds(pl.multiple_of(h * BLK + i * CH, CH), CH)
            gm = pull(z.acc[sp, :] * g1, z.unit1[sp, :], z.inv1[sp, 0:1])
            z.normed[sp, :] = gm
            z.low[sp, :] = gm.astype(bf16)
            return 0

        lax.fori_loop(0, BLK // CH, norm_back, 0)
        for k in range(4):
            g = dot_nt(z.low[hs, :], z.wout[k])
            pair = g[:, 0:LANES].astype(bf16)
            last = jnp.where(left[0:HALF], g[0:HALF, LANES:], pltpu.roll(g[HALF:, LANES:], hd, 1)).astype(bf16)
            if k < 3:
                z.gsend[k, h, 0:BLK, :] = pair
                z.gsend[k, h, BLK:, :] = last
                grad_copy(k, h).start()
            else:
                z.grecv[me, h, 0:BLK, :] = pair
                z.grecv[me, h, BLK:, :] = last
        return 0

    lax.fori_loop(0, 2, rear, 0)

    z.gt[...] = jnp.zeros_like(z.gt)
    z.adp[...] = jnp.zeros_like(z.adp)
    last_block = blocks - 1
    role = lax.rem(cc + yy, 2)

    def place(o):
        og = lax.div(o, 2)
        odd = lax.rem(o, 2)
        return (o + (last_block - 2 * o) * (1 - yy), og + (3 - 2 * og) * (1 - yy), odd + lax.div(o, 4) * (1 - 2 * odd))

    def peer_grad(o):
        return remote(z.gown.at[o], z.gpeer.at[o], z.osem_s.at[o], z.osem_r.at[o], tensor_at(2))

    def part_copy(h):
        return remote(z.psend.at[h], z.precv.at[h], z.psem_s.at[h], z.psem_r.at[h], tensor_at(0))

    def finish(o):
        b, _, _ = place(o)
        span = span_of(b)
        scaled = 2 * width // LANES
        for c in range(pack // LANES):
            t = z.gt[c * LANES:(c + 1) * LANES, span].T
            z.gown[o, :, c * LANES:(c + 1) * LANES] = (t * hd ** -0.5 if c < scaled else t).astype(bf16)
        z.adp[...] += 2.0 * dot(z.yt[3 * width:3 * width + 2 * rank, span], z.gown[o])
        peer_grad(o).start()

    def contract(o):
        _, _, h = place(o)
        peer_grad(o).wait_recv()

        @pl.when(lax.rem(lax.div(o, 2) + role, 2) == 1)
        def _():
            both = dot(z.gown[o], z.weff[...]) + dot(z.gpeer[o], z.weffp[...])

            @pl.when(o < 4)
            def _():
                z.psend[h] = both.astype(bf16)
                part_copy(h).start()

            @pl.when(o >= 4)
            def _():
                hs = span_of(h)
                z.normed[hs, :] = z.normed[hs, :] + both

    def back(n, _):
        @pl.when(n == 0)
        def _():
            grad_copy(0, 0).wait_recv()
            grad_copy(1, 0).wait_recv()

        @pl.when(n == 2)
        def _():
            grad_copy(0, 1).wait_recv()
            grad_copy(1, 1).wait_recv()
            grad_copy(2, 0).wait_recv()
            grad_copy(2, 1).wait_recv()

        d, m4 = lax.div(n, 4), lax.rem(n, 4)
        mid = lax.rem(lax.div(m4 + 1, 2), 2)
        o = n + (1 - d) * mid * (3 - 2 * n)
        qb, g, h2 = place(o)
        span = span_of(qb)
        lo, hi = key_range(qb)
        pair_t = z.grecv[g, h2, 0:BLK, :].astype(f32).T
        last = z.grecv[g, h2, BLK:, :].astype(f32)
        last_t = jnp.concatenate([last, pltpu.roll(last, hd, 1)], axis=0).T[0:hd, :]
        for h in range(heads):
            do = last_t if h == 2 else pair_t[h * hd:(h + 1) * hd, :]
            z.dot_t[h * hd:(h + 1) * hd, :] = do.astype(bf16)
            delta = jnp.sum(do * z.ot[h * hd:(h + 1) * hd, span].astype(f32), axis=0, keepdims=True)
            tail = jnp.zeros((hd, BLK), f32)
            for j, p in enumerate(three_parts(-delta)):
                tail = jnp.where(sub == j, p, tail)
            z.doa[h] = jnp.concatenate([do, tail], axis=0).T.astype(bf16)

        def scores(h, kb):
            keys = span_of(kb)
            p = jnp.exp2(dot_nt(z.qa[h, span, :], z.ka[h, keys, :]) * LOG2E)
            z.pbuf[h] = p.astype(bf16)
            z.dsbuf[h] = (p * dot_nt(z.doa[h], z.va[h, keys, :])).astype(bf16)

        for h in range(heads):
            scores(h, lo)

        def step(kb, _):
            keys = span_of(kb)
            later = jnp.minimum(kb + 1, hi - 1)
            for h in range(heads):
                rq = slice(h * hd, (h + 1) * hd)
                rk = slice(width + h * hd, width + (h + 1) * hd)
                rv = slice(2 * width + h * hd, 2 * width + (h + 1) * hd)
                p, ds = z.pbuf[h], z.dsbuf[h]
                z.gt[rv, keys] += dot(z.dot_t[rq, :], p)
                z.gt[rk, keys] += dot(z.yt[rq, span], ds)
                z.gt[rq, span] += dot_nt(z.yt[rk, keys], ds)
                scores(h, later)
            return 0

        lax.fori_loop(lo, hi, step, 0)

        @pl.when(n >= 2)
        def _():
            finish(n - 2)

        @pl.when(n == 3)
        def _():
            weff_out.wait_recv()

        @pl.when(n >= 3)
        def _():
            contract(n - 3)

        return 0

    lax.fori_loop(0, blocks, back, 0)

    def finish_loop(o, _):
        finish(o)
        return 0

    lax.fori_loop(blocks - 2, blocks, finish_loop, 0)
    wide = 2 * LANES
    z.asend[:, 0:wide] = z.adp[0:rank, 0:wide]
    z.asend[:, wide:] = z.adp[rank:, pack - wide:]
    adapters = [remote(z.asend, z.arecv.at[d], z.asem_s.at[d], z.asem_r.at[d], row_at(d)) for d in range(1, n_dp)]
    for c in adapters:
        c.start()

    def contract_loop(o, _):
        contract(o)
        return 0

    lax.fori_loop(blocks - 3, blocks, contract_loop, 0)
    for h in range(2):
        part_copy(h).wait_recv()
        to = pl.ds(pl.multiple_of(my_rows(h), BLK), BLK)
        z.out[to, :] = z.normed[h * BLK:(h + 1) * BLK, :] + z.precv[h].astype(f32)
    total = z.asend[...]
    for c in adapters:
        c.wait_recv()
    for d in range(1, n_dp):
        total = total + z.arecv[d]
    cols = z.upq.shape[2]
    for base, ref in ((0, z.upq), (wide, z.upv)):
        for h in range(heads):
            at = base + h * hd
            tile = total[:, at // LANES * LANES:(at // LANES + 1) * LANES]
            ref[h] = pltpu.roll(tile, lax.rem(2 * LANES - at % LANES - dp * cols, LANES), 1)[:, 0:cols]

    for v in moves:
        for c in [v.a, v.partner, v.x, v.z, v.second] + v.d:
            c.wait_send()
    weff_out.wait_send()
    for h in range(2):
        for k in range(3):
            ctx_copy(k, h).wait_send()
            grad_copy(k, h).wait_send()
        part_copy(h).wait_send()
    for o in range(blocks):
        peer_grad(o).wait_send()
    for c in adapters:
        c.wait_send()


V = pl.BlockSpec(memory_space=pltpu.VMEM)
S = pl.BlockSpec(memory_space=pltpu.SMEM)
ANY = pl.BlockSpec(memory_space=pl.ANY)


def on_device(n_dp, groups, tokens, seq_lengths, query_weight, key_weight, value_weight, out_weight, ffn_in, ffn_out,
              gain_attn, gain_ffn, query_down, value_down, query_up, value_up, cotangent):
    rows, feat = tokens.shape
    width = query_weight.shape[1]
    rank, heads, hd = query_up.shape
    hidden = ffn_in.shape[1]
    own = rows // groups
    blocks = rows // BLK
    packed = (groups, own // BLK, BLK + HALF, LANES)
    pack = 5 * LANES
    cols = hd // n_dp
    dma = pltpu.SemaphoreType.DMA
    shape = jax.ShapeDtypeStruct
    inputs = [
        ("lens", seq_lengths, S), ("tok_hbm", tokens, ANY), ("cot_hbm", cotangent, ANY),
        ("wq", query_weight.T, V), ("wk", key_weight.T, V), ("wv", value_weight.T, V),
        ("dq", query_down.T, V), ("dv", value_down.T, V), ("uq", query_up.transpose(1, 0, 2), V), ("uv", value_up.transpose(1, 0, 2), V),
        ("ow", out_weight, ANY), ("fi", ffn_in, ANY), ("fo", ffn_out, ANY),
        ("g1", gain_attn.reshape(1, feat), V), ("g2", gain_ffn.reshape(1, feat), V),
    ]
    outputs = [
        ("act", shape((own, feat), bf16)), ("out", shape((own, feat), f32)),
        ("upq", shape((heads, rank, cols), f32)), ("upv", shape((heads, rank, cols), f32)),
    ]
    vm = pltpu.VMEM
    scratch = [
        ("tok", vm((rows, feat), bf16)), ("cot", vm((own, feat), bf16)),
        ("weff", vm((pack, feat), bf16)), ("weffp", vm((pack, feat), bf16)),
        ("qa", vm((heads, rows, LANES), bf16)), ("ka", vm((heads, rows, LANES), bf16)), ("va", vm((heads, rows, LANES), bf16)),
        ("yt", vm((pack, rows), bf16)), ("vt", vm((heads, hd + 16, rows), bf16)), ("ot", vm((width, rows), bf16)),
        ("sbuf", vm((heads, BLK, BLK), f32)), ("oacc", vm((heads, hd + 16, BLK), f32)), ("peak", vm((8, BLK), f32)),
        ("xin", vm((BLK, groups * 2 * LANES), bf16)), ("xsend", vm(packed, bf16)), ("xb", vm(packed, bf16)),
        ("wout", vm((groups, 2 * LANES, feat), bf16)), ("wfi", vm((groups, feat, hidden), bf16)), ("wfo", vm((groups, hidden, feat), bf16)),
        ("normed", vm((own, feat), f32)), ("unit1", vm((own, feat), f32)), ("inv1", vm((own, LANES), f32)),
        ("low", vm((own, feat), bf16)), ("acc", vm((own, feat), f32)), ("gel", vm((groups, own, hidden), bf16)),
        ("actv", vm((2, BLK, hidden), bf16)), ("gsend", vm(packed, bf16)), ("grecv", vm(packed, bf16)),
        ("doa", vm((heads, BLK, LANES), bf16)), ("dot_t", vm((width, BLK), bf16)),
        ("pbuf", vm((heads, BLK, BLK), bf16)), ("dsbuf", vm((heads, BLK, BLK), bf16)),
        ("gt", vm((pack, rows), f32)), ("adp", vm((2 * rank, pack), f32)),
        ("gown", vm((blocks, BLK, pack), bf16)), ("gpeer", vm((blocks, BLK, pack), bf16)),
        ("psend", vm((2, BLK, feat), bf16)), ("precv", vm((2, BLK, feat), bf16)),
        ("asend", vm((rank, 4 * LANES), f32)), ("arecv", vm((n_dp, rank, 4 * LANES), f32)),
        ("lsem", dma((8,))), ("wsem_s", dma((3, 9))), ("wsem_r", dma((3, 9))), ("esem_s", dma((1,))), ("esem_r", dma((1,))),
        ("csem_s", dma((3, 2))), ("csem_r", dma((3, 2))), ("gsem_s", dma((3, 2))), ("gsem_r", dma((3, 2))),
        ("osem_s", dma((blocks,))), ("osem_r", dma((blocks,))), ("psem_s", dma((2,))), ("psem_r", dma((2,))),
        ("asem_s", dma((n_dp,))), ("asem_r", dma((n_dp,))),
    ]
    names = [n for n, _, _ in inputs] + [n for n, _ in outputs] + [n for n, _ in scratch]
    act, grad_input, up_q, up_v = pl.pallas_call(
        functools.partial(layer_kernel, n_dp, heads, hd, names),
        out_shape=tuple(s for _, s in outputs),
        in_specs=[s for _, _, s in inputs],
        out_specs=(V,) * 4,
        scratch_shapes=[s for _, s in scratch],
        compiler_params=pltpu.CompilerParams(vmem_limit_bytes=VMEM_LIMIT, collective_id=0, has_side_effects=True),
        name="layer",
    )(*[a for _, a, _ in inputs])
    return act, grad_input, up_q.transpose(1, 0, 2), up_v.transpose(1, 0, 2)


def solution(mesh):
    in_specs = (
        P("dp", None), P("dp", None), P(None, "tensor"), P(None, "tensor"), P(None, "tensor"), P("tensor", None),
        P(None, "tensor"), P("tensor", None), P(), P(), P(), P(), P(None, "tensor", None), P(None, "tensor", None),
        P("dp", None),
    )
    out_specs = (P(("dp", "tensor"), None), P(("dp", "tensor"), None), P(None, "tensor", "dp"), P(None, "tensor", "dp"))
    return jax.shard_map(
        functools.partial(on_device, mesh.shape["dp"], mesh.shape["tensor"]),
        mesh=mesh, in_specs=in_specs, out_specs=out_specs, check_vma=False,
    )
```

```python
import functools

import jax
import jax.numpy as jnp
from jax import lax
from jax.experimental import pallas as pl
from jax.experimental.pallas import tpu as pltpu
from jax.sharding import PartitionSpec as P

EPSILON = 1e-05
BLOCKED = -1e30
LOG2E = 1.4426950408889634
BLK = 256
HALF = BLK // 2
LANES = 128
REACH = 2
f32 = jnp.float32
bf16 = jnp.bfloat16
VMEM_LIMIT = 59 * 1024 * 1024
MESH = pl.DeviceIdType.MESH
TN = (((0,), (0,)), ((), ()))


def dot(a, b):
    return jnp.dot(a, b, preferred_element_type=f32)


def dot_nt(a, b):
    return lax.dot_general(a, b, (((1,), (1,)), ((), ())), preferred_element_type=f32)


def iota(shape, axis):
    return lax.broadcasted_iota(jnp.int32, shape, axis)


def three_parts(x):
    hi = x.astype(bf16).astype(f32)
    mid = (x - hi).astype(bf16).astype(f32)
    low = (x - hi - mid).astype(bf16).astype(f32)
    return hi, mid, low


def phi_parts(a):
    z = jnp.abs(a)
    t = 1.0 / (1.0 + 0.23164188 * z)
    e = jnp.exp2(a * a * (-0.5 * LOG2E))
    q = t * (0.127414796 + t * (-0.142248368 + t * (0.710706871 + t * (-0.726576014 + t * 0.530702714))))
    tail = q * e
    return jnp.where(a >= 0.0, 1.0 - tail, tail), e


def moments(v):
    mean = jnp.mean(v, axis=-1, keepdims=True)
    c = v - mean
    inv = lax.rsqrt(jnp.mean(c * c, axis=-1, keepdims=True) + EPSILON)
    return c * inv, inv


def pull(w, u, inv):
    return inv * (w - jnp.mean(w, axis=-1, keepdims=True) - u * jnp.mean(w * u, axis=-1, keepdims=True))


class Bag:
    pass


def layer_kernel(n_dp, heads, hd, names, *refs):
    z = Bag()
    for name, ref in zip(names, refs):
        setattr(z, name, ref)
    rows, feat = z.tok.shape
    blocks = rows // BLK
    own = z.out.shape[0]
    per = own // BLK
    width = heads * hd
    slots = z.lens.shape[1]
    rank = z.dq.shape[0]
    pack = z.weff.shape[0]
    part = z.ow.shape[0]
    me = lax.axis_index("tensor")
    dp = lax.axis_index("dp")
    yy, cc = lax.div(me, 2), lax.rem(me, 2)
    px, pz = lax.rem(dp, 2), lax.rem(lax.div(dp, 2), 2)

    def member(k):
        fy = 1 - k // 2
        fc = (k % 2 + k // 2) % 2
        return 2 * lax.rem(yy + fy, 2) + lax.rem(cc + fc, 2)

    def tensor_at(k):
        return {"tensor": member(k)}

    x_peer = {"dp": dp + 1 - 2 * px}
    z_peer = {"dp": dp + 2 - 4 * pz}

    def row_at(d):
        return {"dp": lax.rem(dp + d, n_dp)}

    def remote(src, dst, send, recv, device):
        return pltpu.make_async_remote_copy(src_ref=src, dst_ref=dst, send_sem=send, recv_sem=recv,
                                            device_id=device, device_id_type=MESH)

    per_chunk = rows // 4
    tok_in = [pltpu.make_async_copy(z.tok_hbm.at[pl.ds(j * per_chunk, per_chunk)], z.tok.at[pl.ds(j * per_chunk, per_chunk)],
                                    z.lsem.at[j]) for j in range(4)]
    cot_in = pltpu.make_async_copy(z.cot_hbm.at[pl.ds(pl.multiple_of(me * own, own), own)], z.cot, z.lsem.at[4])
    weights = ((z.ow, z.wout), (z.fi, z.wfi), (z.fo, z.wfo))

    def full(dst, k):
        return dst.at[k, 0:part] if dst is z.wout else dst.at[k]

    own_w = [pltpu.make_async_copy(src, full(dst, 3), z.lsem.at[5 + i]) for i, (src, dst) in enumerate(weights)]
    for c in tok_in + own_w + [cot_in]:
        c.start()
    barrier = pltpu.get_barrier_semaphore()
    for k in range(3):
        pl.semaphore_signal(barrier, inc=1, device_id=tensor_at(k), device_id_type=MESH)
    for d in range(1, n_dp):
        pl.semaphore_signal(barrier, inc=1, device_id=row_at(d), device_id_type=MESH)

    z.weff[width:2 * width, :] = z.wk[...]
    for base, w_ref, d_ref, u_ref in ((0, z.wq, z.dq, z.uq), (2 * width, z.wv, z.dv, z.uv)):
        for h in range(heads):
            low_rank = lax.dot_general(u_ref[h], d_ref[...], TN, preferred_element_type=f32)
            mine = w_ref[h * hd:(h + 1) * hd, :].astype(f32) + 2.0 * low_rank
            z.weff[base + h * hd:base + (h + 1) * hd, :] = mine.astype(bf16)
    downs = jnp.concatenate([z.dq[...].astype(f32), z.dv[...].astype(f32)], axis=0)
    z.weff[3 * width:3 * width + 2 * rank, :] = downs.astype(bf16)
    z.weff[3 * width + 2 * rank:, :] = jnp.zeros((pack - 3 * width - 2 * rank, feat), bf16)
    for h in range(heads):
        z.vt[h, hd:, :] = jnp.ones((z.vt.shape[1] - hd, rows), bf16)
    for k in range(4):
        z.wout[k, part:, :] = jnp.zeros((z.wout.shape[1] - part, feat), bf16)
    pl.semaphore_wait(barrier, 3 + n_dp - 1)

    def quarter(v, k, dx, dz, lo=0, n=None):
        q = 2 * lax.rem(pz + dz, 2) + lax.rem(px + dx, 2)
        return v.dst.at[k, pl.ds(pl.multiple_of(v.base + q * v.n + lo, 16), v.n if n is None else n)]

    partners = [remote(src, full(dst, 2), z.bsem_s.at[i], z.bsem_r.at[i], tensor_at(2)) for i, (src, dst) in enumerate(weights)]
    pieces = [(z.ow, z.wout, 0, part)]
    for src, dst in weights[1:]:
        rows2 = src.shape[0] // 2
        pieces += [(src, dst, 0, rows2), (src, dst, rows2, rows2)]
    moves = []
    for i, (src, dst, base, rows2) in enumerate(pieces):
        v = Bag()
        v.dst, v.base, v.n = dst, base, rows2 // 4
        cut = v.n // 32 * 16
        sem = lambda j, i=i: (z.wsem_s.at[i, j], z.wsem_r.at[i, j])
        here = src.at[pl.ds(pl.multiple_of(base + (2 * pz + px) * v.n, 16), v.n)]
        v.a = remote(here, quarter(v, 0, 0, 0), *sem(0), tensor_at(0))
        v.x = remote(quarter(v, 0, 0, 0), quarter(v, 0, 0, 0), *sem(1), x_peer)
        v.z = remote(quarter(v, 0, 0, 0), quarter(v, 0, 0, 0), *sem(2), z_peer)
        v.far_x = remote(quarter(v, 0, 0, 1, 0, cut), quarter(v, 0, 0, 1, 0, cut), *sem(3), x_peer)
        v.far_z = remote(quarter(v, 0, 1, 0, cut, v.n - cut), quarter(v, 0, 1, 0, cut, v.n - cut), *sem(4), z_peer)
        v.d = [remote(quarter(v, 0, *q), quarter(v, 1, *q), *sem(5 + j), tensor_at(2))
               for j, q in enumerate(((0, 0), (1, 0), (0, 1), (1, 1)))]
        moves.append(v)
    for v in moves:
        v.a.start()
    weff_out = remote(z.weff, z.weffp, z.esem_s.at[0], z.esem_r.at[0], tensor_at(2))
    for c in partners:
        c.start()
    weff_out.start()

    def relay1(i):
        v = moves[i]
        v.a.wait_recv()
        v.x.start()
        v.z.start()
        v.d[0].start()

    def relay2(i):
        v = moves[i]
        v.z.wait_recv()
        v.far_x.start()
        v.x.wait_recv()
        v.far_z.start()
        v.d[2].start()
        v.d[1].start()

    def relay3(i):
        v = moves[i]
        v.far_x.wait_recv()
        v.far_z.wait_recv()
        v.d[3].start()

    def arrive(i):
        for c in moves[i].d:
            c.wait_recv()

    def at(counter, value, *steps):
        @pl.when(counter == value)
        def _():
            for step, i in steps:
                step(i)

    starts, ends = [], []
    total = jnp.int32(0)
    for s in range(slots):
        starts.append(total)
        total = total + z.lens[0, s]
        ends.append(total)
    n_valid = ends[slots - 2]
    lane = iota((1, LANES), 1)
    seg_start = jnp.zeros((1, LANES), jnp.int32)
    seg_end = jnp.zeros((1, LANES), jnp.int32)
    for s in range(slots):
        seg_start = jnp.where(lane == hd + s, starts[s], seg_start)
        seg_end = jnp.where(lane == hd + s, ends[s], seg_end)
    is_mask = (lane >= hd) & (lane < hd + slots)
    extra = jnp.where((lane >= hd + slots) & (lane < hd + slots + 3), 1.0, 0.0)
    ones_v = jnp.where((lane >= hd) & (lane < hd + 3), 1.0, 0.0)
    lanes = iota((BLK, LANES), 1)
    left = lanes < hd

    def span_of(b):
        return pl.ds(pl.multiple_of(b * BLK, BLK), BLK)

    def project(i, _):
        for j in range(4):
            @pl.when(i == j * (blocks // 4))
            def _():
                tok_in[j].wait()
        span = span_of(i)
        y = dot_nt(z.tok[span, :], z.weff[...])
        pos = i * BLK + iota((BLK, LANES), 0)
        mine = (pos >= seg_start) & (pos < seg_end)
        q_mask = jnp.where(mine, 1.0, 0.0)
        k_mask = jnp.where(is_mask & jnp.logical_not(mine), BLOCKED, extra)
        for c in range(pack // LANES):
            z.yt[c * LANES:(c + 1) * LANES, span] = y[:, c * LANES:(c + 1) * LANES].T.astype(bf16)

        def head(n):
            tile = y[:, (n // 2) * LANES:(n // 2 + 1) * LANES]
            return tile if n % 2 == 0 else pltpu.roll(tile, hd, 1)

        for h in range(heads):
            z.qa[h, span, :] = jnp.where(left, head(h) * hd ** -0.5, q_mask).astype(bf16)
            z.ka[h, span, :] = jnp.where(left, head(heads + h), k_mask).astype(bf16)
            z.va[h, span, :] = jnp.where(left, head(2 * heads + h), ones_v).astype(bf16)
            n = (2 * heads + h) * hd
            z.vt[h, 0:hd, span] = z.yt[n:n + hd, span]
        at(i, blocks // 2, (relay1, 0))
        at(i, blocks - 1, (relay1, 1))
        return 0

    lax.fori_loop(0, blocks, project, 0)

    def block_of(g, h):
        return per * g + h + lax.div(g, 2) * (1 - 2 * h)

    def key_range(qb):
        return jnp.maximum(qb - REACH, 0), jnp.minimum(qb + REACH + 1, blocks)

    def ctx_copy(k, h):
        return remote(z.xsend.at[k, h], z.xb.at[k, h], z.csem_s.at[k, h], z.csem_r.at[k, h], tensor_at(k))

    sub = iota((hd, BLK), 0)
    depth = z.vt.shape[1]

    def attend(n, _):
        h2, k2 = lax.div(n, 4), lax.rem(n, 4)
        fy = 1 - lax.div(k2, 2)
        fc = lax.rem(lax.rem(k2, 2) + lax.div(k2, 2), 2)
        g = 2 * lax.rem(yy + fy, 2) + lax.rem(cc + fc, 2)
        qb = block_of(g, h2)
        span = span_of(qb)
        lo, hi = key_range(qb)
        z.oacc[...] = jnp.zeros_like(z.oacc)
        z.peak[...] = jnp.full(z.peak.shape, BLOCKED, f32)

        def score(h, kb):
            z.sbuf[h] = dot_nt(z.ka[h, span_of(kb), :], z.qa[h, span, :])

        for h in range(heads):
            score(h, lo)

        def keys(kb, _):
            later = jnp.minimum(kb + 1, hi - 1)
            for h in range(heads):
                s = z.sbuf[h]
                old = z.peak[h:h + 1, :]
                new = jnp.maximum(old, jnp.max(s, axis=0, keepdims=True))
                p = jnp.exp2((s - new) * LOG2E).astype(bf16)
                z.peak[h:h + 1, :] = new
                scale = jnp.exp2((old - new) * LOG2E)
                z.oacc[h] = z.oacc[h] * scale + dot(z.vt[h, :, span_of(kb)], p)
                score(h, later)
            return 0

        lax.fori_loop(lo, hi, keys, 0)
        outs = []
        for h in range(heads):
            weight = z.oacc[h, hd:hd + 1, :]
            o = z.oacc[h, 0:hd, :] * (1.0 / weight)
            z.ot[h * hd:(h + 1) * hd, span] = o.astype(bf16)
            parts = three_parts(-(z.peak[h:h + 1, :] + jnp.log(weight)))
            tail = jnp.zeros((hd, BLK), f32)
            for j, p in enumerate(parts):
                tail = jnp.where(sub == slots + j, p, tail)
            t = jnp.concatenate([o, tail], axis=0).T
            outs.append(t)
            in_tail = (lanes >= hd + slots) & (lanes < hd + slots + 3)
            z.qa[h, span, :] = jnp.where(in_tail, t, z.qa[h, span, :].astype(f32)).astype(bf16)
        z.xsend[k2, h2, 0:BLK, :] = jnp.where(left, outs[0], pltpu.roll(outs[1], hd, 1)).astype(bf16)
        z.xsend[k2, h2, BLK:, :] = jnp.where(left[0:HALF], outs[2][0:HALF], pltpu.roll(outs[2][HALF:], hd, 1)).astype(bf16)

        @pl.when(k2 < 3)
        def _():
            remote(z.xsend.at[k2, h2], z.xb.at[k2, h2], z.csem_s.at[k2, h2], z.csem_r.at[k2, h2], {"tensor": g}).start()

        at(n, 0, (relay2, 0), (relay1, 2))
        at(n, 1, (relay3, 0), (relay2, 1))
        at(n, 2, (relay1, 3))
        at(n, 3, (relay2, 2), (relay3, 1))
        at(n, 4, (relay1, 4))
        at(n, 5, (relay2, 3), (relay3, 2))
        at(n, 6, (relay2, 4))
        at(n, 7, (relay3, 3))
        return 0

    lax.fori_loop(0, 2 * 4, attend, 0)

    wflat = z.wout.reshape(4 * 2 * LANES, feat)
    g1 = jnp.concatenate([z.g1[i:i + 1, :] for i in range(feat // LANES)], axis=1)
    g2 = jnp.concatenate([z.g2[i:i + 1, :] for i in range(feat // LANES)], axis=1)
    CH = 64

    def my_rows(h):
        return (h + yy * (1 - 2 * h)) * BLK

    def front(h, _):
        hs = span_of(h)

        @pl.when(h == 0)
        def _():
            own_w[0].wait()
            partners[0].wait_recv()
            arrive(0)

        for k in range(3):
            ctx_copy(k, h).wait_recv()
        for k in range(4):
            src = z.xsend if k == 3 else z.xb
            z.xin[:, 2 * k * LANES:(2 * k + 1) * LANES] = src[k, h, 0:BLK, :]
            b = src[k, h, BLK:, :]
            z.xin[0:HALF, (2 * k + 1) * LANES:(2 * k + 2) * LANES] = b
            z.xin[HALF:, (2 * k + 1) * LANES:(2 * k + 2) * LANES] = pltpu.roll(b.astype(f32), hd, 1).astype(bf16)
        z.acc[hs, :] = dot(z.xin[...], wflat[...])
        row0 = me * own + my_rows(h)

        def norm_one(i, _):
            sp = pl.ds(pl.multiple_of(h * BLK + i * CH, CH), CH)
            tp = pl.ds(pl.multiple_of(row0 + i * CH, CH), CH)
            u, inv = moments(z.tok[tp, :].astype(f32) + z.acc[sp, :])
            z.unit1[sp, :] = u
            z.inv1[sp, :] = jnp.broadcast_to(inv, (CH, LANES))
            z.normed[sp, :] = u * g1
            z.low[sp, :] = (u * g1).astype(bf16)
            return 0

        lax.fori_loop(0, BLK // CH, norm_one, 0)

        @pl.when(h == 0)
        def _():
            relay3(4)
            own_w[1].wait()
            own_w[2].wait()
            partners[1].wait_recv()
            partners[2].wait_recv()

        pre = dot(z.low[hs, :], z.wfi[3])
        for k in (3, 2):
            later = dot(z.low[hs, :], z.wfi[2]) if k == 3 else None
            cdf, e = phi_parts(pre)
            z.gel[k, hs, :] = (cdf + pre * e * 0.3989422804014327).astype(bf16)
            out = dot((pre * cdf).astype(bf16), z.wfo[k])
            z.acc[hs, :] = out if k == 3 else z.acc[hs, :] + out
            pre = later

        return 0

    lax.fori_loop(0, 2, front, 0)
    cot_in.wait()

    def grad_copy(k, h):
        return remote(z.gsend.at[k, h], z.grecv.at[me, h], z.gsem_s.at[k, h], z.gsem_r.at[k, h], tensor_at(k))

    def rear(h, _):
        hs = span_of(h)

        @pl.when(h == 0)
        def _():
            arrive(1)
            arrive(2)

        pre = dot(z.low[hs, :], z.wfi[0])
        for k in range(2):
            later = dot(z.low[hs, :], z.wfi[1]) if k == 0 else None
            cdf, e = phi_parts(pre)
            z.gel[k, hs, :] = (cdf + pre * e * 0.3989422804014327).astype(bf16)
            z.actv[k] = (pre * cdf).astype(bf16)
            pre = later

        @pl.when(h == 0)
        def _():
            arrive(3)
            arrive(4)

        z.acc[hs, :] += dot(z.actv[0], z.wfo[0]) + dot(z.actv[1], z.wfo[1])
        row0 = my_rows(h)

        def norm_two(i, _):
            sp = pl.ds(pl.multiple_of(h * BLK + i * CH, CH), CH)
            tp = pl.ds(pl.multiple_of(row0 + i * CH, CH), CH)
            u, inv = moments(z.normed[sp, :] + z.acc[sp, :])
            pos = me * own + row0 + i * CH + iota((CH, 1), 0)
            valid = jnp.where(pos < n_valid, 1.0, 0.0)
            z.act[tp, :] = (u * g2 * valid).astype(bf16)
            gm = pull(z.cot[tp, :].astype(f32) * valid * g2, u, inv)
            z.acc[sp, :] = gm
            z.low[sp, :] = gm.astype(bf16)
            return 0

        lax.fori_loop(0, BLK // CH, norm_two, 0)
        ga = dot_nt(z.low[hs, :], z.wfo[0])
        for k in range(4):
            later = dot_nt(z.low[hs, :], z.wfo[k + 1]) if k < 3 else None
            z.acc[hs, :] += dot_nt((ga * z.gel[k, hs, :].astype(f32)).astype(bf16), z.wfi[k])
            ga = later

        def norm_back(i, _):
            sp = pl.ds(pl.multiple_of(h * BLK + i * CH, CH), CH)
            gm = pull(z.acc[sp, :] * g1, z.unit1[sp, :], z.inv1[sp, 0:1])
            z.normed[sp, :] = gm
            z.low[sp, :] = gm.astype(bf16)
            return 0

        lax.fori_loop(0, BLK // CH, norm_back, 0)
        for k in range(4):
            g = dot_nt(z.low[hs, :], z.wout[k])
            pair = g[:, 0:LANES].astype(bf16)
            last = jnp.where(left[0:HALF], g[0:HALF, LANES:], pltpu.roll(g[HALF:, LANES:], hd, 1)).astype(bf16)
            if k < 3:
                z.gsend[k, h, 0:BLK, :] = pair
                z.gsend[k, h, BLK:, :] = last
                grad_copy(k, h).start()
            else:
                z.grecv[me, h, 0:BLK, :] = pair
                z.grecv[me, h, BLK:, :] = last
        return 0

    lax.fori_loop(0, 2, rear, 0)

    z.gt[...] = jnp.zeros_like(z.gt)
    z.adp[...] = jnp.zeros_like(z.adp)
    last_block = blocks - 1
    role = lax.rem(cc + yy, 2)

    def place(o):
        og = lax.div(o, 2)
        odd = lax.rem(o, 2)
        return (o + (last_block - 2 * o) * (1 - yy), og + (3 - 2 * og) * (1 - yy), odd + lax.div(o, 4) * (1 - 2 * odd))

    def peer_grad(o):
        return remote(z.gown.at[o], z.gpeer.at[o], z.osem_s.at[o], z.osem_r.at[o], tensor_at(2))

    def part_copy(h):
        return remote(z.psend.at[h], z.precv.at[h], z.psem_s.at[h], z.psem_r.at[h], tensor_at(0))

    def finish(o):
        b, _, _ = place(o)
        span = span_of(b)
        scaled = 2 * width // LANES
        for c in range(pack // LANES):
            t = z.gt[c * LANES:(c + 1) * LANES, span].T
            z.gown[o, :, c * LANES:(c + 1) * LANES] = (t * hd ** -0.5 if c < scaled else t).astype(bf16)
        z.adp[...] += 2.0 * dot(z.yt[3 * width:3 * width + 2 * rank, span], z.gown[o])
        peer_grad(o).start()

    def contract(o):
        _, _, h = place(o)
        peer_grad(o).wait_recv()

        @pl.when(lax.rem(lax.div(o, 2) + role, 2) == 1)
        def _():
            both = dot(z.gown[o], z.weff[...]) + dot(z.gpeer[o], z.weffp[...])

            @pl.when(o < 4)
            def _():
                z.psend[h] = both.astype(bf16)
                part_copy(h).start()

            @pl.when(o >= 4)
            def _():
                hs = span_of(h)
                z.normed[hs, :] = z.normed[hs, :] + both

    def back(n, _):
        @pl.when(n == 0)
        def _():
            grad_copy(0, 0).wait_recv()
            grad_copy(1, 0).wait_recv()

        @pl.when(n == 2)
        def _():
            grad_copy(0, 1).wait_recv()
            grad_copy(1, 1).wait_recv()
            grad_copy(2, 0).wait_recv()
            grad_copy(2, 1).wait_recv()

        d, m4 = lax.div(n, 4), lax.rem(n, 4)
        mid = lax.rem(lax.div(m4 + 1, 2), 2)
        o = n + (1 - d) * mid * (3 - 2 * n)
        qb, g, h2 = place(o)
        span = span_of(qb)
        lo, hi = key_range(qb)
        pair_t = z.grecv[g, h2, 0:BLK, :].astype(f32).T
        last = z.grecv[g, h2, BLK:, :].astype(f32)
        last_t = jnp.concatenate([last, pltpu.roll(last, hd, 1)], axis=0).T[0:hd, :]
        for h in range(heads):
            do = last_t if h == 2 else pair_t[h * hd:(h + 1) * hd, :]
            z.dot_t[h * hd:(h + 1) * hd, :] = do.astype(bf16)
            delta = jnp.sum(do * z.ot[h * hd:(h + 1) * hd, span].astype(f32), axis=0, keepdims=True)
            tail = jnp.zeros((hd, BLK), f32)
            for j, p in enumerate(three_parts(-delta)):
                tail = jnp.where(sub == j, p, tail)
            z.doa[h] = jnp.concatenate([do, tail], axis=0).T.astype(bf16)

        def scores(h, kb):
            keys = span_of(kb)
            p = jnp.exp2(dot_nt(z.qa[h, span, :], z.ka[h, keys, :]) * LOG2E)
            z.pbuf[h] = p.astype(bf16)
            z.dsbuf[h] = (p * dot_nt(z.doa[h], z.va[h, keys, :])).astype(bf16)

        for h in range(heads):
            scores(h, lo)

        def step(kb, _):
            keys = span_of(kb)
            later = jnp.minimum(kb + 1, hi - 1)
            for h in range(heads):
                rq = slice(h * hd, (h + 1) * hd)
                rk = slice(width + h * hd, width + (h + 1) * hd)
                rv = slice(2 * width + h * hd, 2 * width + (h + 1) * hd)
                p, ds = z.pbuf[h], z.dsbuf[h]
                z.gt[rv, keys] += dot(z.dot_t[rq, :], p)
                z.gt[rk, keys] += dot(z.yt[rq, span], ds)
                z.gt[rq, span] += dot_nt(z.yt[rk, keys], ds)
                scores(h, later)
            return 0

        lax.fori_loop(lo, hi, step, 0)

        @pl.when(n >= 2)
        def _():
            finish(n - 2)

        @pl.when(n == 3)
        def _():
            weff_out.wait_recv()

        @pl.when(n >= 3)
        def _():
            contract(n - 3)

        return 0

    lax.fori_loop(0, blocks, back, 0)

    def finish_loop(o, _):
        finish(o)
        return 0

    lax.fori_loop(blocks - 2, blocks, finish_loop, 0)
    wide = 2 * LANES
    z.asend[:, 0:wide] = z.adp[0:rank, 0:wide]
    z.asend[:, wide:] = z.adp[rank:, pack - wide:]
    adapters = [remote(z.asend, z.arecv.at[d], z.asem_s.at[d], z.asem_r.at[d], row_at(d)) for d in range(1, n_dp)]
    for c in adapters:
        c.start()

    def contract_loop(o, _):
        contract(o)
        return 0

    lax.fori_loop(blocks - 3, blocks, contract_loop, 0)
    for h in range(2):
        part_copy(h).wait_recv()
        to = pl.ds(pl.multiple_of(my_rows(h), BLK), BLK)
        z.out[to, :] = z.normed[h * BLK:(h + 1) * BLK, :] + z.precv[h].astype(f32)
    total = z.asend[...]
    for c in adapters:
        c.wait_recv()
    for d in range(1, n_dp):
        total = total + z.arecv[d]
    cols = z.upq.shape[2]
    for base, ref in ((0, z.upq), (wide, z.upv)):
        for h in range(heads):
            at = base + h * hd
            tile = total[:, at // LANES * LANES:(at // LANES + 1) * LANES]
            ref[h] = pltpu.roll(tile, lax.rem(2 * LANES - at % LANES - dp * cols, LANES), 1)[:, 0:cols]

    for v in moves:
        for c in [v.a, v.x, v.z, v.far_x, v.far_z] + v.d:
            c.wait_send()
    for c in partners:
        c.wait_send()
    weff_out.wait_send()
    for h in range(2):
        for k in range(3):
            ctx_copy(k, h).wait_send()
            grad_copy(k, h).wait_send()
        part_copy(h).wait_send()
    for o in range(blocks):
        peer_grad(o).wait_send()
    for c in adapters:
        c.wait_send()


def emit_kernel(act, out, upq, upv, act_hbm, out_hbm, upq_hbm, upv_hbm, sem):
    copies = [pltpu.make_async_copy(src, dst, sem.at[i]) for i, (src, dst) in
              enumerate(((out, out_hbm), (act, act_hbm), (upq, upq_hbm), (upv, upv_hbm)))]
    for c in copies:
        c.start()
    for c in copies:
        c.wait()


V = pl.BlockSpec(memory_space=pltpu.VMEM)
S = pl.BlockSpec(memory_space=pltpu.SMEM)
ANY = pl.BlockSpec(memory_space=pl.ANY)


def on_device(n_dp, groups, tokens, seq_lengths, query_weight, key_weight, value_weight, out_weight, ffn_in, ffn_out,
              gain_attn, gain_ffn, query_down, value_down, query_up, value_up, cotangent):
    rows, feat = tokens.shape
    width = query_weight.shape[1]
    rank, heads, hd = query_up.shape
    hidden = ffn_in.shape[1]
    own = rows // groups
    blocks = rows // BLK
    packed = (groups, own // BLK, BLK + HALF, LANES)
    pack = 5 * LANES
    cols = hd // n_dp
    dma = pltpu.SemaphoreType.DMA
    shape = jax.ShapeDtypeStruct
    inputs = [
        ("lens", seq_lengths, S), ("tok_hbm", tokens, ANY), ("cot_hbm", cotangent, ANY),
        ("wq", query_weight.T, V), ("wk", key_weight.T, V), ("wv", value_weight.T, V),
        ("dq", query_down.T, V), ("dv", value_down.T, V), ("uq", query_up.transpose(1, 0, 2), V), ("uv", value_up.transpose(1, 0, 2), V),
        ("ow", out_weight, ANY), ("fi", ffn_in, ANY), ("fo", ffn_out, ANY),
        ("g1", gain_attn.reshape(feat // LANES, LANES), V), ("g2", gain_ffn.reshape(feat // LANES, LANES), V),
    ]
    outputs = [
        ("act", shape((own, feat), bf16)), ("out", shape((own, feat), f32)),
        ("upq", shape((heads, rank, cols), f32)), ("upv", shape((heads, rank, cols), f32)),
    ]
    vm = pltpu.VMEM
    scratch = [
        ("tok", vm((rows, feat), bf16)), ("cot", vm((own, feat), bf16)),
        ("weff", vm((pack, feat), bf16)), ("weffp", vm((pack, feat), bf16)),
        ("qa", vm((heads, rows, LANES), bf16)), ("ka", vm((heads, rows, LANES), bf16)), ("va", vm((heads, rows, LANES), bf16)),
        ("yt", vm((pack, rows), bf16)), ("vt", vm((heads, hd + 16, rows), bf16)), ("ot", vm((width, rows), bf16)),
        ("sbuf", vm((heads, BLK, BLK), f32)), ("oacc", vm((heads, hd + 16, BLK), f32)), ("peak", vm((8, BLK), f32)),
        ("xin", vm((BLK, groups * 2 * LANES), bf16)), ("xsend", vm(packed, bf16)), ("xb", vm(packed, bf16)),
        ("wout", vm((groups, 2 * LANES, feat), bf16)), ("wfi", vm((groups, feat, hidden), bf16)), ("wfo", vm((groups, hidden, feat), bf16)),
        ("normed", vm((own, feat), f32)), ("unit1", vm((own, feat), f32)), ("inv1", vm((own, LANES), f32)),
        ("low", vm((own, feat), bf16)), ("acc", vm((own, feat), f32)), ("gel", vm((groups, own, hidden), bf16)),
        ("actv", vm((2, BLK, hidden), bf16)), ("gsend", vm(packed, bf16)), ("grecv", vm(packed, bf16)),
        ("doa", vm((heads, BLK, LANES), bf16)), ("dot_t", vm((width, BLK), bf16)),
        ("pbuf", vm((heads, BLK, BLK), bf16)), ("dsbuf", vm((heads, BLK, BLK), bf16)),
        ("gt", vm((pack, rows), f32)), ("adp", vm((2 * rank, pack), f32)),
        ("gown", vm((blocks, BLK, pack), bf16)), ("gpeer", vm((blocks, BLK, pack), bf16)),
        ("psend", vm((2, BLK, feat), bf16)), ("precv", vm((2, BLK, feat), bf16)),
        ("asend", vm((rank, 4 * LANES), f32)), ("arecv", vm((n_dp, rank, 4 * LANES), f32)),
        ("lsem", dma((8,))), ("wsem_s", dma((5, 9))), ("wsem_r", dma((5, 9))), ("bsem_s", dma((3,))), ("bsem_r", dma((3,))), ("esem_s", dma((1,))), ("esem_r", dma((1,))),
        ("csem_s", dma((3, 2))), ("csem_r", dma((3, 2))), ("gsem_s", dma((3, 2))), ("gsem_r", dma((3, 2))),
        ("osem_s", dma((blocks,))), ("osem_r", dma((blocks,))), ("psem_s", dma((2,))), ("psem_r", dma((2,))),
        ("asem_s", dma((n_dp,))), ("asem_r", dma((n_dp,))),
    ]
    names = [n for n, _, _ in inputs] + [n for n, _ in outputs] + [n for n, _ in scratch]
    results = pl.pallas_call(
        functools.partial(layer_kernel, n_dp, heads, hd, names),
        out_shape=tuple(vm(s.shape, s.dtype) for _, s in outputs),
        in_specs=[s for _, _, s in inputs],
        out_specs=(V,) * 4,
        scratch_shapes=[s for _, s in scratch],
        compiler_params=pltpu.CompilerParams(vmem_limit_bytes=VMEM_LIMIT, collective_id=0, has_side_effects=True),
        name="layer",
    )(*[a for _, a, _ in inputs])
    act, grad_input, up_q, up_v = pl.pallas_call(
        emit_kernel,
        out_shape=tuple(s for _, s in outputs),
        in_specs=[V] * 4,
        out_specs=(ANY,) * 4,
        scratch_shapes=[dma((4,))],
        compiler_params=pltpu.CompilerParams(vmem_limit_bytes=4 * 1024 * 1024),
        name="emit",
    )(*results)
    return act, grad_input, up_q.transpose(1, 0, 2), up_v.transpose(1, 0, 2)


def solution(mesh):
    in_specs = (
        P("dp", None), P("dp", None), P(None, "tensor"), P(None, "tensor"), P(None, "tensor"), P("tensor", None),
        P(None, "tensor"), P("tensor", None), P(), P(), P(), P(), P(None, "tensor", None), P(None, "tensor", None),
        P("dp", None),
    )
    out_specs = (P(("dp", "tensor"), None), P(("dp", "tensor"), None), P(None, "tensor", "dp"), P(None, "tensor", "dp"))
    return jax.shard_map(
        functools.partial(on_device, mesh.shape["dp"], mesh.shape["tensor"]),
        mesh=mesh, in_specs=in_specs, out_specs=out_specs, check_vma=False,
    )
```

```python
import functools

import jax
import jax.numpy as jnp
from jax import lax
from jax.experimental import pallas as pl
from jax.experimental.pallas import tpu as pltpu
from jax.sharding import PartitionSpec as P

EPSILON = 1e-05
BLOCKED = -1e30
LOG2E = 1.4426950408889634
BLK = 256
HALF = BLK // 2
LANES = 128
REACH = 2
f32 = jnp.float32
bf16 = jnp.bfloat16
VMEM_LIMIT = 59 * 1024 * 1024
MESH = pl.DeviceIdType.MESH
TN = (((0,), (0,)), ((), ()))


def dot(a, b):
    return jnp.dot(a, b, preferred_element_type=f32)


def dot_nt(a, b):
    return lax.dot_general(a, b, (((1,), (1,)), ((), ())), preferred_element_type=f32)


def iota(shape, axis):
    return lax.broadcasted_iota(jnp.int32, shape, axis)


def three_parts(x):
    hi = x.astype(bf16).astype(f32)
    mid = (x - hi).astype(bf16).astype(f32)
    low = (x - hi - mid).astype(bf16).astype(f32)
    return hi, mid, low


def phi_parts(a):
    z = jnp.abs(a)
    t = 1.0 / (1.0 + 0.23164188 * z)
    e = jnp.exp2(a * a * (-0.5 * LOG2E))
    q = t * (0.127414796 + t * (-0.142248368 + t * (0.710706871 + t * (-0.726576014 + t * 0.530702714))))
    tail = q * e
    return jnp.where(a >= 0.0, 1.0 - tail, tail), e


def moments(v):
    mean = jnp.mean(v, axis=-1, keepdims=True)
    c = v - mean
    inv = lax.rsqrt(jnp.mean(c * c, axis=-1, keepdims=True) + EPSILON)
    return c * inv, inv


def pull(w, u, inv):
    return inv * (w - jnp.mean(w, axis=-1, keepdims=True) - u * jnp.mean(w * u, axis=-1, keepdims=True))


class Bag:
    pass


def layer_kernel(n_dp, heads, hd, names, *refs):
    z = Bag()
    for name, ref in zip(names, refs):
        setattr(z, name, ref)
    rows, feat = z.tok.shape
    blocks = rows // BLK
    own = z.out.shape[0]
    per = own // BLK
    width = heads * hd
    slots = z.lens.shape[1]
    rank = z.dq.shape[0]
    pack = z.weff.shape[0]
    part = z.ow.shape[0]
    me = lax.axis_index("tensor")
    dp = lax.axis_index("dp")
    yy, cc = lax.div(me, 2), lax.rem(me, 2)
    px, pz = lax.rem(dp, 2), lax.rem(lax.div(dp, 2), 2)

    def member(k):
        fy = 1 - k // 2
        fc = (k % 2 + k // 2) % 2
        return 2 * lax.rem(yy + fy, 2) + lax.rem(cc + fc, 2)

    def tensor_at(k):
        return {"tensor": member(k)}

    x_peer = {"dp": dp + 1 - 2 * px}
    z_peer = {"dp": dp + 2 - 4 * pz}

    def row_at(d):
        return {"dp": lax.rem(dp + d, n_dp)}

    def remote(src, dst, send, recv, device):
        return pltpu.make_async_remote_copy(src_ref=src, dst_ref=dst, send_sem=send, recv_sem=recv,
                                            device_id=device, device_id_type=MESH)

    per_chunk = rows // 4
    tok_in = [pltpu.make_async_copy(z.tok_hbm.at[pl.ds(j * per_chunk, per_chunk)], z.tok.at[pl.ds(j * per_chunk, per_chunk)],
                                    z.lsem.at[j]) for j in range(4)]
    cot_in = pltpu.make_async_copy(z.cot_hbm.at[pl.ds(pl.multiple_of(me * own, own), own)], z.cot, z.lsem.at[4])
    weights = ((z.ow, z.wout), (z.fi, z.wfi), (z.fo, z.wfo))

    def full(dst, k):
        return dst.at[k, 0:part] if dst is z.wout else dst.at[k]

    own_w = [pltpu.make_async_copy(src, full(dst, 3), z.lsem.at[5 + i]) for i, (src, dst) in enumerate(weights)]
    for c in tok_in + own_w + [cot_in]:
        c.start()
    barrier = pltpu.get_barrier_semaphore()
    for k in range(3):
        pl.semaphore_signal(barrier, inc=1, device_id=tensor_at(k), device_id_type=MESH)
    for d in range(1, n_dp):
        pl.semaphore_signal(barrier, inc=1, device_id=row_at(d), device_id_type=MESH)

    z.weff[width:2 * width, :] = z.wk[...]
    for base, w_ref, d_ref, u_ref in ((0, z.wq, z.dq, z.uq), (2 * width, z.wv, z.dv, z.uv)):
        for h in range(heads):
            low_rank = lax.dot_general(u_ref[h], d_ref[...], TN, preferred_element_type=f32)
            mine = w_ref[h * hd:(h + 1) * hd, :].astype(f32) + 2.0 * low_rank
            z.weff[base + h * hd:base + (h + 1) * hd, :] = mine.astype(bf16)
    downs = jnp.concatenate([z.dq[...].astype(f32), z.dv[...].astype(f32)], axis=0)
    z.weff[3 * width:3 * width + 2 * rank, :] = downs.astype(bf16)
    z.weff[3 * width + 2 * rank:, :] = jnp.zeros((pack - 3 * width - 2 * rank, feat), bf16)
    for h in range(heads):
        z.vt[h, hd:, :] = jnp.ones((z.vt.shape[1] - hd, rows), bf16)
    for k in range(4):
        z.wout[k, part:, :] = jnp.zeros((z.wout.shape[1] - part, feat), bf16)
    pl.semaphore_wait(barrier, 3 + n_dp - 1)

    def quarter(v, k, dx, dz, lo=0, n=None):
        q = 2 * lax.rem(pz + dz, 2) + lax.rem(px + dx, 2)
        return v.dst.at[k, pl.ds(pl.multiple_of(v.base + q * v.n + lo, 16), v.n if n is None else n)]

    partners = [remote(src, full(dst, 2), z.bsem_s.at[i], z.bsem_r.at[i], tensor_at(2)) for i, (src, dst) in enumerate(weights)]
    pieces = [(z.ow, z.wout, 0, part)]
    for src, dst in weights[1:]:
        rows2 = src.shape[0] // 2
        pieces += [(src, dst, 0, rows2), (src, dst, rows2, rows2)]
    moves = []
    for i, (src, dst, base, rows2) in enumerate(pieces):
        v = Bag()
        v.dst, v.base, v.n = dst, base, rows2 // 4
        cut = v.n // 32 * 16
        sem = lambda j, i=i: (z.wsem_s.at[i, j], z.wsem_r.at[i, j])
        here = src.at[pl.ds(pl.multiple_of(base + (2 * pz + px) * v.n, 16), v.n)]
        v.a = remote(here, quarter(v, 0, 0, 0), *sem(0), tensor_at(0))
        v.x = remote(quarter(v, 0, 0, 0), quarter(v, 0, 0, 0), *sem(1), x_peer)
        v.z = remote(quarter(v, 0, 0, 0), quarter(v, 0, 0, 0), *sem(2), z_peer)
        v.far_x = remote(quarter(v, 0, 0, 1, 0, cut), quarter(v, 0, 0, 1, 0, cut), *sem(3), x_peer)
        v.far_z = remote(quarter(v, 0, 1, 0, cut, v.n - cut), quarter(v, 0, 1, 0, cut, v.n - cut), *sem(4), z_peer)
        v.d = [remote(quarter(v, 0, *q), quarter(v, 1, *q), *sem(5 + j), tensor_at(2))
               for j, q in enumerate(((0, 0), (1, 0), (0, 1), (1, 1)))]
        moves.append(v)
    for v in moves:
        v.a.start()
    weff_out = remote(z.weff, z.weffp, z.esem_s.at[0], z.esem_r.at[0], tensor_at(2))
    for c in partners:
        c.start()
    weff_out.start()

    def relay1(i):
        v = moves[i]
        v.a.wait_recv()
        v.x.start()
        v.z.start()
        v.d[0].start()

    def relay2(i):
        v = moves[i]
        v.z.wait_recv()
        v.far_x.start()
        v.x.wait_recv()
        v.far_z.start()
        v.d[2].start()
        v.d[1].start()

    def relay3(i):
        v = moves[i]
        v.far_x.wait_recv()
        v.far_z.wait_recv()
        v.d[3].start()

    def arrive(i):
        for c in moves[i].d:
            c.wait_recv()

    def at(counter, value, *steps):
        def once(_, carry):
            for step, i in steps:
                step(i)
            return carry

        lax.fori_loop(0, jnp.where(counter == value, 1, 0), once, 0)

    starts, ends = [], []
    total = jnp.int32(0)
    for s in range(slots):
        starts.append(total)
        total = total + z.lens[0, s]
        ends.append(total)
    n_valid = ends[slots - 2]
    lane = iota((1, LANES), 1)
    seg_start = jnp.zeros((1, LANES), jnp.int32)
    seg_end = jnp.zeros((1, LANES), jnp.int32)
    for s in range(slots):
        seg_start = jnp.where(lane == hd + s, starts[s], seg_start)
        seg_end = jnp.where(lane == hd + s, ends[s], seg_end)
    is_mask = (lane >= hd) & (lane < hd + slots)
    extra = jnp.where((lane >= hd + slots) & (lane < hd + slots + 3), 1.0, 0.0)
    ones_v = jnp.where((lane >= hd) & (lane < hd + 3), 1.0, 0.0)
    lanes = iota((BLK, LANES), 1)
    left = lanes < hd

    def span_of(b):
        return pl.ds(pl.multiple_of(b * BLK, BLK), BLK)

    def project(i, _):
        for j in range(4):
            @pl.when(i == j * (blocks // 4))
            def _():
                tok_in[j].wait()
        span = span_of(i)
        y = dot_nt(z.tok[span, :], z.weff[...])
        z.gt[:, span] = jnp.zeros((pack, BLK), f32)
        pos = i * BLK + iota((BLK, LANES), 0)
        mine = (pos >= seg_start) & (pos < seg_end)
        q_mask = jnp.where(mine, 1.0, 0.0)
        k_mask = jnp.where(is_mask & jnp.logical_not(mine), BLOCKED, extra)
        for c in range(pack // LANES):
            z.yt[c * LANES:(c + 1) * LANES, span] = y[:, c * LANES:(c + 1) * LANES].T.astype(bf16)

        def head(n):
            tile = y[:, (n // 2) * LANES:(n // 2 + 1) * LANES]
            return tile if n % 2 == 0 else pltpu.roll(tile, hd, 1)

        for h in range(heads):
            z.qa[h, span, :] = jnp.where(left, head(h) * hd ** -0.5, q_mask).astype(bf16)
            z.ka[h, span, :] = jnp.where(left, head(heads + h), k_mask).astype(bf16)
            z.va[h, span, :] = jnp.where(left, head(2 * heads + h), ones_v).astype(bf16)
            n = (2 * heads + h) * hd
            z.vt[h, 0:hd, span] = z.yt[n:n + hd, span]
        at(i, blocks // 2, (relay1, 0))
        at(i, blocks - 1, (relay1, 1))
        return 0

    lax.fori_loop(0, blocks, project, 0)

    def block_of(g, h):
        return per * g + h + lax.div(g, 2) * (1 - 2 * h)

    win = min(2 * REACH + 1, blocks)

    def window(qb):
        return jnp.minimum(jnp.maximum(qb - REACH, 0), blocks - win)

    def ctx_copy(k, h):
        return remote(z.xsend.at[k, h], z.xb.at[k, h], z.csem_s.at[k, h], z.csem_r.at[k, h], tensor_at(k))

    sub = iota((hd, BLK), 0)

    def attend(n, _):
        h2, k2 = lax.div(n, 4), lax.rem(n, 4)
        fy = 1 - lax.div(k2, 2)
        fc = lax.rem(lax.rem(k2, 2) + lax.div(k2, 2), 2)
        g = 2 * lax.rem(yy + fy, 2) + lax.rem(cc + fc, 2)
        qb = block_of(g, h2)
        span = span_of(qb)
        lo = window(qb)

        def score(h):
            top = None
            for j in range(win):
                s = dot_nt(z.ka[h, span_of(lo + j), :], z.qa[h, span, :])
                z.sbuf[h, j] = s
                best = jnp.max(s.reshape(BLK // 8, 8, BLK), axis=0)
                top = best if top is None else jnp.maximum(top, best)
            return jnp.max(top, axis=0, keepdims=True)

        peaks = [score(0)]
        outs = []
        for h in range(heads):
            if h + 1 < heads:
                peaks.append(score(h + 1))
            acc = None
            for j in range(win):
                p = jnp.exp2((z.sbuf[h, j] - peaks[h]) * LOG2E).astype(bf16)
                o = dot(z.vt[h, :, span_of(lo + j)], p)
                acc = o if acc is None else acc + o
            weight = acc[hd:hd + 1, :]
            o = acc[0:hd, :] * (1.0 / weight)
            z.ot[h * hd:(h + 1) * hd, span] = o.astype(bf16)
            parts = three_parts(-(peaks[h] + jnp.log(weight)))
            tail = jnp.zeros((hd, BLK), f32)
            for j, p in enumerate(parts):
                tail = jnp.where(sub == slots + j, p, tail)
            t = jnp.concatenate([o, tail], axis=0).T
            outs.append(t)
            in_tail = (lanes >= hd + slots) & (lanes < hd + slots + 3)
            z.qa[h, span, :] = jnp.where(in_tail, t, z.qa[h, span, :].astype(f32)).astype(bf16)
        z.xsend[k2, h2, 0:BLK, :] = jnp.where(left, outs[0], pltpu.roll(outs[1], hd, 1)).astype(bf16)
        z.xsend[k2, h2, BLK:, :] = jnp.where(left[0:HALF], outs[2][0:HALF], pltpu.roll(outs[2][HALF:], hd, 1)).astype(bf16)

        @pl.when(k2 < 3)
        def _():
            remote(z.xsend.at[k2, h2], z.xb.at[k2, h2], z.csem_s.at[k2, h2], z.csem_r.at[k2, h2], {"tensor": g}).start()

        at(n, 0, (relay2, 0))
        at(n, 1, (relay1, 2))
        at(n, 2, (relay2, 1))
        at(n, 3, (relay1, 3))
        at(n, 5, (relay1, 4), (relay2, 2))
        return 0

    lax.fori_loop(0, 2 * 4, attend, 0)

    wflat = z.wout.reshape(4 * 2 * LANES, feat)
    g1 = jnp.concatenate([z.g1[i:i + 1, :] for i in range(feat // LANES)], axis=1)
    g2 = jnp.concatenate([z.g2[i:i + 1, :] for i in range(feat // LANES)], axis=1)
    CH = 64

    def my_rows(h):
        return (h + yy * (1 - 2 * h)) * BLK

    def front(h, _):
        hs = span_of(h)

        @pl.when(h == 0)
        def _():
            own_w[0].wait()
            partners[0].wait_recv()
            relay3(0)
            arrive(0)

        for k in range(3):
            ctx_copy(k, h).wait_recv()
        for k in range(4):
            src = z.xsend if k == 3 else z.xb
            z.xin[:, 2 * k * LANES:(2 * k + 1) * LANES] = src[k, h, 0:BLK, :]
            b = src[k, h, BLK:, :]
            z.xin[0:HALF, (2 * k + 1) * LANES:(2 * k + 2) * LANES] = b
            z.xin[HALF:, (2 * k + 1) * LANES:(2 * k + 2) * LANES] = pltpu.roll(b.astype(f32), hd, 1).astype(bf16)
        z.acc[hs, :] = dot(z.xin[...], wflat[...])
        row0 = me * own + my_rows(h)

        def norm_one(i, _):
            sp = pl.ds(pl.multiple_of(h * BLK + i * CH, CH), CH)
            tp = pl.ds(pl.multiple_of(row0 + i * CH, CH), CH)
            u, inv = moments(z.tok[tp, :].astype(f32) + z.acc[sp, :])
            z.unit1[sp, :] = u
            z.inv1[sp, :] = jnp.broadcast_to(inv, (CH, LANES))
            z.normed[sp, :] = u * g1
            z.low[sp, :] = (u * g1).astype(bf16)
            return 0

        lax.fori_loop(0, BLK // CH, norm_one, 0)

        @pl.when(h == 0)
        def _():
            relay2(3)
            own_w[1].wait()
            own_w[2].wait()
            partners[1].wait_recv()
            partners[2].wait_recv()

        at(h, 1, (relay3, 1), (relay2, 4), (relay3, 2))
        pre = dot(z.low[hs, :], z.wfi[3])
        for k in (3, 2):
            later = dot(z.low[hs, :], z.wfi[2]) if k == 3 else None
            cdf, e = phi_parts(pre)
            z.gel[k, hs, :] = (cdf + pre * e * 0.3989422804014327).astype(bf16)
            out = dot((pre * cdf).astype(bf16), z.wfo[k])
            z.acc[hs, :] = out if k == 3 else z.acc[hs, :] + out
            pre = later

        return 0

    lax.fori_loop(0, 2, front, 0)
    cot_in.wait()

    def grad_copy(k, h):
        return remote(z.gsend.at[k, h], z.grecv.at[me, h], z.gsem_s.at[k, h], z.gsem_r.at[k, h], tensor_at(k))

    def rear(h, _):
        hs = span_of(h)

        @pl.when(h == 0)
        def _():
            arrive(1)
            arrive(2)

        pre = dot(z.low[hs, :], z.wfi[0])
        for k in range(2):
            later = dot(z.low[hs, :], z.wfi[1]) if k == 0 else None
            cdf, e = phi_parts(pre)
            z.gel[k, hs, :] = (cdf + pre * e * 0.3989422804014327).astype(bf16)
            z.actv[k] = (pre * cdf).astype(bf16)
            pre = later

        @pl.when(h == 0)
        def _():
            relay3(3)
            relay3(4)
            arrive(3)
            arrive(4)

        z.acc[hs, :] += dot(z.actv[0], z.wfo[0]) + dot(z.actv[1], z.wfo[1])
        row0 = my_rows(h)

        def norm_two(i, _):
            sp = pl.ds(pl.multiple_of(h * BLK + i * CH, CH), CH)
            tp = pl.ds(pl.multiple_of(row0 + i * CH, CH), CH)
            u, inv = moments(z.normed[sp, :] + z.acc[sp, :])
            pos = me * own + row0 + i * CH + iota((CH, 1), 0)
            valid = jnp.where(pos < n_valid, 1.0, 0.0)
            z.act[tp, :] = (u * g2 * valid).astype(bf16)
            gm = pull(z.cot[tp, :].astype(f32) * valid * g2, u, inv)
            z.acc[sp, :] = gm
            z.low[sp, :] = gm.astype(bf16)
            return 0

        lax.fori_loop(0, BLK // CH, norm_two, 0)
        ga = dot_nt(z.low[hs, :], z.wfo[0])
        for k in range(4):
            later = dot_nt(z.low[hs, :], z.wfo[k + 1]) if k < 3 else None
            z.acc[hs, :] += dot_nt((ga * z.gel[k, hs, :].astype(f32)).astype(bf16), z.wfi[k])
            ga = later

        def norm_back(i, _):
            sp = pl.ds(pl.multiple_of(h * BLK + i * CH, CH), CH)
            gm = pull(z.acc[sp, :] * g1, z.unit1[sp, :], z.inv1[sp, 0:1])
            z.normed[sp, :] = gm
            z.low[sp, :] = gm.astype(bf16)
            return 0

        lax.fori_loop(0, BLK // CH, norm_back, 0)
        later = dot_nt(z.low[hs, :], z.wout[0])
        for k in range(4):
            g = later
            if k < 3:
                later = dot_nt(z.low[hs, :], z.wout[k + 1])
            pair = g[:, 0:LANES].astype(bf16)
            last = jnp.where(left[0:HALF], g[0:HALF, LANES:], pltpu.roll(g[HALF:, LANES:], hd, 1)).astype(bf16)
            if k < 3:
                z.gsend[k, h, 0:BLK, :] = pair
                z.gsend[k, h, BLK:, :] = last
                grad_copy(k, h).start()
            else:
                z.grecv[me, h, 0:BLK, :] = pair
                z.grecv[me, h, BLK:, :] = last
        return 0

    lax.fori_loop(0, 2, rear, 0)

    z.adp[...] = jnp.zeros_like(z.adp)
    last_block = blocks - 1
    role = lax.rem(cc + yy, 2)

    def place(o):
        og = lax.div(o, 2)
        odd = lax.rem(o, 2)
        return (o + (last_block - 2 * o) * (1 - yy), og + (3 - 2 * og) * (1 - yy), odd + lax.div(o, 4) * (1 - 2 * odd))

    def peer_grad(o):
        return remote(z.gown.at[o], z.gpeer.at[o], z.osem_s.at[o], z.osem_r.at[o], tensor_at(2))

    def part_copy(h):
        return remote(z.psend.at[h], z.precv.at[h], z.psem_s.at[h], z.psem_r.at[h], tensor_at(0))

    def finish(o):
        b, _, _ = place(o)
        span = span_of(b)
        scaled = 2 * width // LANES
        for c in range(pack // LANES):
            t = z.gt[c * LANES:(c + 1) * LANES, span].T
            z.gown[o, :, c * LANES:(c + 1) * LANES] = (t * hd ** -0.5 if c < scaled else t).astype(bf16)
        z.adp[...] += 2.0 * dot(z.yt[3 * width:3 * width + 2 * rank, span], z.gown[o])
        peer_grad(o).start()

    def contract(o):
        _, _, h = place(o)
        peer_grad(o).wait_recv()

        @pl.when(lax.rem(lax.div(o, 2) + role, 2) == 1)
        def _():
            both = dot(z.gown[o], z.weff[...]) + dot(z.gpeer[o], z.weffp[...])

            @pl.when(o < 4)
            def _():
                z.psend[h] = both.astype(bf16)
                part_copy(h).start()

            @pl.when(o >= 4)
            def _():
                hs = span_of(h)
                z.normed[hs, :] = z.normed[hs, :] + both

    def back(n, _):
        @pl.when(n == 0)
        def _():
            grad_copy(0, 0).wait_recv()
            grad_copy(1, 0).wait_recv()

        @pl.when(n == 2)
        def _():
            grad_copy(0, 1).wait_recv()
            grad_copy(1, 1).wait_recv()
            grad_copy(2, 0).wait_recv()
            grad_copy(2, 1).wait_recv()

        d, m4 = lax.div(n, 4), lax.rem(n, 4)
        mid = lax.rem(lax.div(m4 + 1, 2), 2)
        o = n + (1 - d) * mid * (3 - 2 * n)
        qb, g, h2 = place(o)
        span = span_of(qb)
        lo = window(qb)
        pair_t = z.grecv[g, h2, 0:BLK, :].astype(f32).T
        last = z.grecv[g, h2, BLK:, :].astype(f32)
        last_t = jnp.concatenate([last, pltpu.roll(last, hd, 1)], axis=0).T[0:hd, :]
        for h in range(heads):
            do = last_t if h == 2 else pair_t[h * hd:(h + 1) * hd, :]
            z.dot_t[h * hd:(h + 1) * hd, :] = do.astype(bf16)
            delta = jnp.sum(do * z.ot[h * hd:(h + 1) * hd, span].astype(f32), axis=0, keepdims=True)
            tail = jnp.zeros((hd, BLK), f32)
            for j, p in enumerate(three_parts(-delta)):
                tail = jnp.where(sub == j, p, tail)
            z.doa[h] = jnp.concatenate([do, tail], axis=0).T.astype(bf16)

        def scores(h, j):
            keys = span_of(lo + j)
            p = jnp.exp2(dot_nt(z.qa[h, span, :], z.ka[h, keys, :]) * LOG2E)
            z.pbuf[h, j] = p.astype(bf16)
            z.dsbuf[h, :, j * BLK:(j + 1) * BLK] = (p * dot_nt(z.doa[h], z.va[h, keys, :])).astype(bf16)

        for h in range(heads):
            scores(h, 0)
        for j in range(win):
            keys = span_of(lo + j)
            for h in range(heads):
                rq = slice(h * hd, (h + 1) * hd)
                rk = slice(width + h * hd, width + (h + 1) * hd)
                rv = slice(2 * width + h * hd, 2 * width + (h + 1) * hd)
                if j + 1 < win:
                    scores(h, j + 1)
                z.gt[rv, keys] += dot(z.dot_t[rq, :], z.pbuf[h, j])
                z.gt[rk, keys] += dot(z.yt[rq, span], z.dsbuf[h, :, j * BLK:(j + 1) * BLK])
                if j + 1 == win:
                    around = pl.ds(pl.multiple_of(lo * BLK, BLK), win * BLK)
                    z.gt[rq, span] = dot_nt(z.yt[rk, around], z.dsbuf[h])

        @pl.when(n >= 2)
        def _():
            finish(n - 2)

        @pl.when(n == 3)
        def _():
            weff_out.wait_recv()

        @pl.when(n >= 3)
        def _():
            contract(n - 3)

        return 0

    lax.fori_loop(0, blocks, back, 0)

    def finish_loop(o, _):
        finish(o)
        return 0

    lax.fori_loop(blocks - 2, blocks, finish_loop, 0)
    wide = 2 * LANES
    z.asend[:, 0:wide] = z.adp[0:rank, 0:wide]
    z.asend[:, wide:] = z.adp[rank:, pack - wide:]
    adapters = [remote(z.asend, z.arecv.at[d], z.asem_s.at[d], z.asem_r.at[d], row_at(d)) for d in range(1, n_dp)]
    for c in adapters:
        c.start()

    def contract_loop(o, _):
        contract(o)
        return 0

    lax.fori_loop(blocks - 3, blocks, contract_loop, 0)
    for v in moves:
        for c in [v.a, v.x, v.z, v.far_x, v.far_z] + v.d:
            c.wait_send()
    for c in partners:
        c.wait_send()
    for h in range(2):
        part_copy(h).wait_recv()
        to = pl.ds(pl.multiple_of(my_rows(h), BLK), BLK)
        z.out[to, :] = z.normed[h * BLK:(h + 1) * BLK, :] + z.precv[h].astype(f32)
    total = z.asend[...]
    for c in adapters:
        c.wait_recv()
    for d in range(1, n_dp):
        total = total + z.arecv[d]
    cols = z.upq.shape[2]
    for base, ref in ((0, z.upq), (wide, z.upv)):
        for h in range(heads):
            at = base + h * hd
            tile = total[:, at // LANES * LANES:(at // LANES + 1) * LANES]
            ref[h] = pltpu.roll(tile, lax.rem(2 * LANES - at % LANES - dp * cols, LANES), 1)[:, 0:cols]

    weff_out.wait_send()
    for h in range(2):
        for k in range(3):
            ctx_copy(k, h).wait_send()
            grad_copy(k, h).wait_send()
        part_copy(h).wait_send()
    for o in range(blocks):
        peer_grad(o).wait_send()
    for c in adapters:
        c.wait_send()


def emit_kernel(act, out, upq, upv, act_hbm, out_hbm, upq_hbm, upv_hbm, sem):
    copies = [pltpu.make_async_copy(src, dst, sem.at[i]) for i, (src, dst) in
              enumerate(((out, out_hbm), (act, act_hbm), (upq, upq_hbm), (upv, upv_hbm)))]
    for c in copies:
        c.start()
    for c in copies:
        c.wait()


V = pl.BlockSpec(memory_space=pltpu.VMEM)
S = pl.BlockSpec(memory_space=pltpu.SMEM)
ANY = pl.BlockSpec(memory_space=pl.ANY)


def on_device(n_dp, groups, tokens, seq_lengths, query_weight, key_weight, value_weight, out_weight, ffn_in, ffn_out,
              gain_attn, gain_ffn, query_down, value_down, query_up, value_up, cotangent):
    rows, feat = tokens.shape
    width = query_weight.shape[1]
    rank, heads, hd = query_up.shape
    hidden = ffn_in.shape[1]
    own = rows // groups
    blocks = rows // BLK
    packed = (groups, own // BLK, BLK + HALF, LANES)
    pack = 5 * LANES
    cols = hd // n_dp
    win = min(2 * REACH + 1, blocks)
    dma = pltpu.SemaphoreType.DMA
    shape = jax.ShapeDtypeStruct
    inputs = [
        ("lens", seq_lengths, S), ("tok_hbm", tokens, ANY), ("cot_hbm", cotangent, ANY),
        ("wq", query_weight.T, V), ("wk", key_weight.T, V), ("wv", value_weight.T, V),
        ("dq", query_down.T, V), ("dv", value_down.T, V), ("uq", query_up.transpose(1, 0, 2), V), ("uv", value_up.transpose(1, 0, 2), V),
        ("ow", out_weight, ANY), ("fi", ffn_in, ANY), ("fo", ffn_out, ANY),
        ("g1", gain_attn.reshape(feat // LANES, LANES), V), ("g2", gain_ffn.reshape(feat // LANES, LANES), V),
    ]
    outputs = [
        ("act", shape((own, feat), bf16)), ("out", shape((own, feat), f32)),
        ("upq", shape((heads, rank, cols), f32)), ("upv", shape((heads, rank, cols), f32)),
    ]
    vm = pltpu.VMEM
    scratch = [
        ("tok", vm((rows, feat), bf16)), ("cot", vm((own, feat), bf16)),
        ("weff", vm((pack, feat), bf16)), ("weffp", vm((pack, feat), bf16)),
        ("qa", vm((heads, rows, LANES), bf16)), ("ka", vm((heads, rows, LANES), bf16)), ("va", vm((heads, rows, LANES), bf16)),
        ("yt", vm((pack, rows), bf16)), ("vt", vm((heads, hd + 16, rows), bf16)), ("ot", vm((width, rows), bf16)),
        ("sbuf", vm((heads, win, BLK, BLK), f32)),
        ("xin", vm((BLK, groups * 2 * LANES), bf16)), ("xsend", vm(packed, bf16)), ("xb", vm(packed, bf16)),
        ("wout", vm((groups, 2 * LANES, feat), bf16)), ("wfi", vm((groups, feat, hidden), bf16)), ("wfo", vm((groups, hidden, feat), bf16)),
        ("normed", vm((own, feat), f32)), ("unit1", vm((own, feat), f32)), ("inv1", vm((own, LANES), f32)),
        ("low", vm((own, feat), bf16)), ("acc", vm((own, feat), f32)), ("gel", vm((groups, own, hidden), bf16)),
        ("actv", vm((2, BLK, hidden), bf16)), ("gsend", vm(packed, bf16)), ("grecv", vm(packed, bf16)),
        ("doa", vm((heads, BLK, LANES), bf16)), ("dot_t", vm((width, BLK), bf16)),
        ("pbuf", vm((heads, win, BLK, BLK), bf16)), ("dsbuf", vm((heads, BLK, win * BLK), bf16)),
        ("gt", vm((pack, rows), f32)), ("adp", vm((2 * rank, pack), f32)),
        ("gown", vm((blocks, BLK, pack), bf16)), ("gpeer", vm((blocks, BLK, pack), bf16)),
        ("psend", vm((2, BLK, feat), bf16)), ("precv", vm((2, BLK, feat), bf16)),
        ("asend", vm((rank, 4 * LANES), f32)), ("arecv", vm((n_dp, rank, 4 * LANES), f32)),
        ("lsem", dma((8,))), ("wsem_s", dma((5, 9))), ("wsem_r", dma((5, 9))), ("bsem_s", dma((3,))), ("bsem_r", dma((3,))), ("esem_s", dma((1,))), ("esem_r", dma((1,))),
        ("csem_s", dma((3, 2))), ("csem_r", dma((3, 2))), ("gsem_s", dma((3, 2))), ("gsem_r", dma((3, 2))),
        ("osem_s", dma((blocks,))), ("osem_r", dma((blocks,))), ("psem_s", dma((2,))), ("psem_r", dma((2,))),
        ("asem_s", dma((n_dp,))), ("asem_r", dma((n_dp,))),
    ]
    names = [n for n, _, _ in inputs] + [n for n, _ in outputs] + [n for n, _ in scratch]
    results = pl.pallas_call(
        functools.partial(layer_kernel, n_dp, heads, hd, names),
        out_shape=tuple(vm(s.shape, s.dtype) for _, s in outputs),
        in_specs=[s for _, _, s in inputs],
        out_specs=(V,) * 4,
        scratch_shapes=[s for _, s in scratch],
        compiler_params=pltpu.CompilerParams(vmem_limit_bytes=VMEM_LIMIT, collective_id=0, has_side_effects=True),
        name="layer",
    )(*[a for _, a, _ in inputs])
    act, grad_input, up_q, up_v = pl.pallas_call(
        emit_kernel,
        out_shape=tuple(s for _, s in outputs),
        in_specs=[V] * 4,
        out_specs=(ANY,) * 4,
        scratch_shapes=[dma((4,))],
        compiler_params=pltpu.CompilerParams(vmem_limit_bytes=4 * 1024 * 1024),
        name="emit",
    )(*results)
    return act, grad_input, up_q.transpose(1, 0, 2), up_v.transpose(1, 0, 2)


def solution(mesh):
    in_specs = (
        P("dp", None), P("dp", None), P(None, "tensor"), P(None, "tensor"), P(None, "tensor"), P("tensor", None),
        P(None, "tensor"), P("tensor", None), P(), P(), P(), P(), P(None, "tensor", None), P(None, "tensor", None),
        P("dp", None),
    )
    out_specs = (P(("dp", "tensor"), None), P(("dp", "tensor"), None), P(None, "tensor", "dp"), P(None, "tensor", "dp"))
    return jax.shard_map(
        functools.partial(on_device, mesh.shape["dp"], mesh.shape["tensor"]),
        mesh=mesh, in_specs=in_specs, out_specs=out_specs, check_vma=False,
    )
```

```python
import functools

import jax
import jax.numpy as jnp
from jax import lax
from jax.experimental import pallas as pl
from jax.experimental.pallas import tpu as pltpu
from jax.sharding import PartitionSpec as P

EPSILON = 1e-05
BLOCKED = -1e30
LOG2E = 1.4426950408889634
BLK = 256
HALF = BLK // 2
LANES = 128
REACH = 2
f32 = jnp.float32
bf16 = jnp.bfloat16
VMEM_LIMIT = 59 * 1024 * 1024
MESH = pl.DeviceIdType.MESH
TN = (((0,), (0,)), ((), ()))


def dot(a, b):
    return jnp.dot(a, b, preferred_element_type=f32)


def dot_nt(a, b):
    return lax.dot_general(a, b, (((1,), (1,)), ((), ())), preferred_element_type=f32)


def iota(shape, axis):
    return lax.broadcasted_iota(jnp.int32, shape, axis)


def three_parts(x):
    hi = x.astype(bf16).astype(f32)
    mid = (x - hi).astype(bf16).astype(f32)
    low = (x - hi - mid).astype(bf16).astype(f32)
    return hi, mid, low


def phi_parts(a):
    z = jnp.abs(a)
    t = 1.0 / (1.0 + 0.23164188 * z)
    e = jnp.exp2(a * a * (-0.5 * LOG2E))
    q = t * (0.127414796 + t * (-0.142248368 + t * (0.710706871 + t * (-0.726576014 + t * 0.530702714))))
    tail = q * e
    return jnp.where(a >= 0.0, 1.0 - tail, tail), e


def moments(v):
    mean = jnp.mean(v, axis=-1, keepdims=True)
    c = v - mean
    inv = lax.rsqrt(jnp.mean(c * c, axis=-1, keepdims=True) + EPSILON)
    return c * inv, inv


def pull(w, u, inv):
    return inv * (w - jnp.mean(w, axis=-1, keepdims=True) - u * jnp.mean(w * u, axis=-1, keepdims=True))


class Bag:
    pass


def layer_kernel(n_dp, heads, hd, names, *refs):
    z = Bag()
    for name, ref in zip(names, refs):
        setattr(z, name, ref)
    rows, feat = z.tok.shape
    blocks = rows // BLK
    own = z.out.shape[0]
    per = own // BLK
    width = heads * hd
    slots = z.lens.shape[1]
    rank = z.dq.shape[0]
    pack = z.weff.shape[0] // 2
    part = z.ow.shape[0]
    me = lax.axis_index("tensor")
    dp = lax.axis_index("dp")
    yy, cc = lax.div(me, 2), lax.rem(me, 2)
    px, pz = lax.rem(dp, 2), lax.rem(lax.div(dp, 2), 2)

    def member(k):
        fy = 1 - k // 2
        fc = (k % 2 + k // 2) % 2
        return 2 * lax.rem(yy + fy, 2) + lax.rem(cc + fc, 2)

    def tensor_at(k):
        return {"tensor": member(k)}

    x_peer = {"dp": dp + 1 - 2 * px}
    z_peer = {"dp": dp + 2 - 4 * pz}

    def row_at(d):
        return {"dp": lax.rem(dp + d, n_dp)}

    def remote(src, dst, send, recv, device):
        return pltpu.make_async_remote_copy(src_ref=src, dst_ref=dst, send_sem=send, recv_sem=recv,
                                            device_id=device, device_id_type=MESH)

    per_chunk = rows // 4
    tok_in = [pltpu.make_async_copy(z.tok_hbm.at[pl.ds(j * per_chunk, per_chunk)], z.tok.at[pl.ds(j * per_chunk, per_chunk)],
                                    z.lsem.at[j]) for j in range(4)]
    cot_in = pltpu.make_async_copy(z.cot_hbm.at[pl.ds(pl.multiple_of(me * own, own), own)], z.cot, z.lsem.at[4])
    weights = ((z.ow, z.wout), (z.fi, z.wfi), (z.fo, z.wfo))

    def full(dst, k):
        return dst.at[k, 0:part] if dst is z.wout else dst.at[k]

    own_w = [pltpu.make_async_copy(src, full(dst, 3), z.lsem.at[5 + i]) for i, (src, dst) in enumerate(weights)]
    for c in tok_in + own_w + [cot_in]:
        c.start()
    barrier = pltpu.get_barrier_semaphore()
    for k in range(3):
        pl.semaphore_signal(barrier, inc=1, device_id=tensor_at(k), device_id_type=MESH)
    for d in range(1, n_dp):
        pl.semaphore_signal(barrier, inc=1, device_id=row_at(d), device_id_type=MESH)

    z.weff[width:2 * width, :] = z.wk[...]
    for base, w_ref, d_ref, u_ref in ((0, z.wq, z.dq, z.uq), (2 * width, z.wv, z.dv, z.uv)):
        for h in range(heads):
            low_rank = lax.dot_general(u_ref[h], d_ref[...], TN, preferred_element_type=f32)
            mine = w_ref[h * hd:(h + 1) * hd, :].astype(f32) + 2.0 * low_rank
            z.weff[base + h * hd:base + (h + 1) * hd, :] = mine.astype(bf16)
    downs = jnp.concatenate([z.dq[...].astype(f32), z.dv[...].astype(f32)], axis=0)
    z.weff[3 * width:3 * width + 2 * rank, :] = downs.astype(bf16)
    z.weff[3 * width + 2 * rank:pack, :] = jnp.zeros((pack - 3 * width - 2 * rank, feat), bf16)
    for h in range(heads):
        z.vt[h, hd:, :] = jnp.ones((z.vt.shape[1] - hd, rows), bf16)
    for k in range(4):
        z.wout[k, part:, :] = jnp.zeros((z.wout.shape[1] - part, feat), bf16)
    pl.semaphore_wait(barrier, 3 + n_dp - 1)

    def quarter(v, k, dx, dz, lo=0, n=None):
        q = 2 * lax.rem(pz + dz, 2) + lax.rem(px + dx, 2)
        return v.dst.at[k, pl.ds(pl.multiple_of(v.base + q * v.n + lo, 16), v.n if n is None else n)]

    partners = [remote(src, full(dst, 2), z.bsem_s.at[i], z.bsem_r.at[i], tensor_at(2)) for i, (src, dst) in enumerate(weights)]
    pieces = [(z.ow, z.wout, 0, part)]
    for src, dst in weights[1:]:
        rows2 = src.shape[0] // 2
        pieces += [(src, dst, 0, rows2), (src, dst, rows2, rows2)]
    moves = []
    for i, (src, dst, base, rows2) in enumerate(pieces):
        v = Bag()
        v.dst, v.base, v.n = dst, base, rows2 // 4
        cut = v.n // 32 * 16
        sem = lambda j, i=i: (z.wsem_s.at[i, j], z.wsem_r.at[i, j])
        here = src.at[pl.ds(pl.multiple_of(base + (2 * pz + px) * v.n, 16), v.n)]
        v.a = remote(here, quarter(v, 0, 0, 0), *sem(0), tensor_at(0))
        v.x = remote(quarter(v, 0, 0, 0), quarter(v, 0, 0, 0), *sem(1), x_peer)
        v.z = remote(quarter(v, 0, 0, 0), quarter(v, 0, 0, 0), *sem(2), z_peer)
        v.far_x = remote(quarter(v, 0, 0, 1, 0, cut), quarter(v, 0, 0, 1, 0, cut), *sem(3), x_peer)
        v.far_z = remote(quarter(v, 0, 1, 0, cut, v.n - cut), quarter(v, 0, 1, 0, cut, v.n - cut), *sem(4), z_peer)
        v.d = [remote(quarter(v, 0, *q), quarter(v, 1, *q), *sem(5 + j), tensor_at(2))
               for j, q in enumerate(((0, 0), (1, 0), (0, 1), (1, 1)))]
        moves.append(v)
    for v in moves:
        v.a.start()
    weff_out = remote(z.weff.at[0:pack], z.weff.at[pack:2 * pack], z.esem_s.at[0], z.esem_r.at[0], tensor_at(2))
    for c in partners:
        c.start()
    weff_out.start()

    def relay1(i):
        v = moves[i]
        v.a.wait_recv()
        v.x.start()
        v.z.start()
        v.d[0].start()

    def relay2(i):
        v = moves[i]
        v.z.wait_recv()
        v.far_x.start()
        v.x.wait_recv()
        v.far_z.start()
        v.d[2].start()
        v.d[1].start()

    def relay3(i):
        v = moves[i]
        v.far_x.wait_recv()
        v.far_z.wait_recv()
        v.d[3].start()

    def arrive(i):
        for c in moves[i].d:
            c.wait_recv()

    def at(counter, value, *steps):
        def once(_, carry):
            for step, i in steps:
                step(i)
            return carry

        lax.fori_loop(0, jnp.where(counter == value, 1, 0), once, 0)

    starts, ends = [], []
    total = jnp.int32(0)
    for s in range(slots):
        starts.append(total)
        total = total + z.lens[0, s]
        ends.append(total)
    n_valid = ends[slots - 2]
    lane = iota((1, LANES), 1)
    seg_start = jnp.zeros((1, LANES), jnp.int32)
    seg_end = jnp.zeros((1, LANES), jnp.int32)
    for s in range(slots):
        seg_start = jnp.where(lane == hd + s, starts[s], seg_start)
        seg_end = jnp.where(lane == hd + s, ends[s], seg_end)
    is_mask = (lane >= hd) & (lane < hd + slots)
    extra = jnp.where((lane >= hd + slots) & (lane < hd + slots + 3), 1.0, 0.0)
    ones_v = jnp.where((lane >= hd) & (lane < hd + 3), 1.0, 0.0)
    lanes = iota((BLK, LANES), 1)
    left = lanes < hd

    def span_of(b):
        return pl.ds(pl.multiple_of(b * BLK, BLK), BLK)

    def project(i, _):
        for j in range(4):
            @pl.when(i == j * (blocks // 4))
            def _():
                tok_in[j].wait()
        span = span_of(i)
        y = dot_nt(z.tok[span, :], z.weff[0:pack, :])
        z.gt[:, span] = jnp.zeros((pack, BLK), f32)
        pos = i * BLK + iota((BLK, LANES), 0)
        mine = (pos >= seg_start) & (pos < seg_end)
        q_mask = jnp.where(mine, 1.0, 0.0)
        k_mask = jnp.where(is_mask & jnp.logical_not(mine), BLOCKED, extra)
        for c in range(pack // LANES):
            z.yt[c * LANES:(c + 1) * LANES, span] = y[:, c * LANES:(c + 1) * LANES].T.astype(bf16)

        def head(n):
            tile = y[:, (n // 2) * LANES:(n // 2 + 1) * LANES]
            return tile if n % 2 == 0 else pltpu.roll(tile, hd, 1)

        for h in range(heads):
            z.qa[h, span, :] = jnp.where(left, head(h) * hd ** -0.5, q_mask).astype(bf16)
            z.ka[h, span, :] = jnp.where(left, head(heads + h), k_mask).astype(bf16)
            z.va[h, span, :] = jnp.where(left, head(2 * heads + h), ones_v).astype(bf16)
            n = (2 * heads + h) * hd
            z.vt[h, 0:hd, span] = z.yt[n:n + hd, span]
        at(i, blocks // 2, (relay1, 0))
        at(i, blocks - 1, (relay1, 1))
        return 0

    lax.fori_loop(0, blocks, project, 0)

    def block_of(g, h):
        return per * g + h + lax.div(g, 2) * (1 - 2 * h)

    win = min(2 * REACH + 1, blocks)

    def window(qb):
        return jnp.minimum(jnp.maximum(qb - REACH, 0), blocks - win)

    def ctx_copy(k, h):
        return remote(z.xsend.at[k, h], z.xb.at[k, h], z.csem_s.at[k, h], z.csem_r.at[k, h], tensor_at(k))

    sub = iota((hd, BLK), 0)

    def attend(n, _):
        h2, k2 = lax.div(n, 4), lax.rem(n, 4)
        fy = 1 - lax.div(k2, 2)
        fc = lax.rem(lax.rem(k2, 2) + lax.div(k2, 2), 2)
        g = 2 * lax.rem(yy + fy, 2) + lax.rem(cc + fc, 2)
        qb = block_of(g, h2)
        span = span_of(qb)
        lo = window(qb)

        def score(h):
            top = None
            for j in range(win):
                s = dot_nt(z.ka[h, span_of(lo + j), :], z.qa[h, span, :])
                z.sbuf[h, j] = s
                best = jnp.max(s.reshape(BLK // 8, 8, BLK), axis=0)
                top = best if top is None else jnp.maximum(top, best)
            return jnp.max(top, axis=0, keepdims=True)

        peaks = [score(0)]
        outs = []
        for h in range(heads):
            if h + 1 < heads:
                peaks.append(score(h + 1))
            acc = None
            for j in range(win):
                p = jnp.exp2((z.sbuf[h, j] - peaks[h]) * LOG2E).astype(bf16)
                o = dot(z.vt[h, :, span_of(lo + j)], p)
                acc = o if acc is None else acc + o
            weight = acc[hd:hd + 1, :]
            o = acc[0:hd, :] * (1.0 / weight)
            z.ot[h * hd:(h + 1) * hd, span] = o.astype(bf16)
            parts = three_parts(-(peaks[h] + jnp.log(weight)))
            tail = jnp.zeros((hd, BLK), f32)
            for j, p in enumerate(parts):
                tail = jnp.where(sub == slots + j, p, tail)
            t = jnp.concatenate([o, tail], axis=0).T
            outs.append(t)
            in_tail = (lanes >= hd + slots) & (lanes < hd + slots + 3)
            z.qa[h, span, :] = jnp.where(in_tail, t, z.qa[h, span, :].astype(f32)).astype(bf16)
        z.xsend[k2, h2, 0:BLK, :] = jnp.where(left, outs[0], pltpu.roll(outs[1], hd, 1)).astype(bf16)
        z.xsend[k2, h2, BLK:, :] = jnp.where(left[0:HALF], outs[2][0:HALF], pltpu.roll(outs[2][HALF:], hd, 1)).astype(bf16)

        @pl.when(k2 < 3)
        def _():
            remote(z.xsend.at[k2, h2], z.xb.at[k2, h2], z.csem_s.at[k2, h2], z.csem_r.at[k2, h2], {"tensor": g}).start()

        at(n, 0, (relay2, 0))
        at(n, 1, (relay1, 2))
        at(n, 2, (relay2, 1))
        at(n, 3, (relay1, 3))
        at(n, 5, (relay1, 4), (relay2, 2))
        return 0

    lax.fori_loop(0, 2 * 4, attend, 0)

    wflat = z.wout.reshape(4 * 2 * LANES, feat)
    g1 = jnp.concatenate([z.g1[i:i + 1, :] for i in range(feat // LANES)], axis=1)
    g2 = jnp.concatenate([z.g2[i:i + 1, :] for i in range(feat // LANES)], axis=1)
    CH = 64

    def my_rows(h):
        return (h + yy * (1 - 2 * h)) * BLK

    def front(h, _):
        hs = span_of(h)

        @pl.when(h == 0)
        def _():
            own_w[0].wait()
            partners[0].wait_recv()
            relay3(0)
            arrive(0)

        for k in range(3):
            ctx_copy(k, h).wait_recv()
        for k in range(4):
            src = z.xsend if k == 3 else z.xb
            z.xin[:, 2 * k * LANES:(2 * k + 1) * LANES] = src[k, h, 0:BLK, :]
            b = src[k, h, BLK:, :]
            z.xin[0:HALF, (2 * k + 1) * LANES:(2 * k + 2) * LANES] = b
            z.xin[HALF:, (2 * k + 1) * LANES:(2 * k + 2) * LANES] = pltpu.roll(b.astype(f32), hd, 1).astype(bf16)
        z.acc[hs, :] = dot(z.xin[...], wflat[...])
        row0 = me * own + my_rows(h)

        def norm_one(i, _):
            sp = pl.ds(pl.multiple_of(h * BLK + i * CH, CH), CH)
            tp = pl.ds(pl.multiple_of(row0 + i * CH, CH), CH)
            u, inv = moments(z.tok[tp, :].astype(f32) + z.acc[sp, :])
            z.unit1[sp, :] = u
            z.inv1[sp, :] = jnp.broadcast_to(inv, (CH, LANES))
            z.normed[sp, :] = u * g1
            z.low[sp, :] = (u * g1).astype(bf16)
            return 0

        lax.fori_loop(0, BLK // CH, norm_one, 0)

        @pl.when(h == 0)
        def _():
            relay2(3)
            own_w[1].wait()
            own_w[2].wait()
            partners[1].wait_recv()
            partners[2].wait_recv()

        at(h, 1, (relay3, 1), (relay2, 4), (relay3, 2))
        pre = dot(z.low[hs, :], z.wfi[3])
        for k in (3, 2):
            later = dot(z.low[hs, :], z.wfi[2]) if k == 3 else None
            cdf, e = phi_parts(pre)
            z.gel[k, hs, :] = (cdf + pre * e * 0.3989422804014327).astype(bf16)
            out = dot((pre * cdf).astype(bf16), z.wfo[k])
            z.acc[hs, :] = out if k == 3 else z.acc[hs, :] + out
            pre = later

        return 0

    lax.fori_loop(0, 2, front, 0)
    cot_in.wait()

    def grad_copy(k, h):
        return remote(z.gsend.at[k, h], z.grecv.at[me, h], z.gsem_s.at[k, h], z.gsem_r.at[k, h], tensor_at(k))

    def rear(h, _):
        hs = span_of(h)

        @pl.when(h == 0)
        def _():
            arrive(1)
            arrive(2)

        pre = dot(z.low[hs, :], z.wfi[0])
        for k in range(2):
            later = dot(z.low[hs, :], z.wfi[1]) if k == 0 else None
            cdf, e = phi_parts(pre)
            z.gel[k, hs, :] = (cdf + pre * e * 0.3989422804014327).astype(bf16)
            z.actv[k] = (pre * cdf).astype(bf16)
            pre = later

        @pl.when(h == 0)
        def _():
            relay3(3)
            relay3(4)

        z.acc[hs, :] += dot(z.actv[0], z.wfo[0])

        @pl.when(h == 0)
        def _():
            arrive(3)
            arrive(4)

        z.acc[hs, :] += dot(z.actv[1], z.wfo[1])
        row0 = my_rows(h)

        def norm_two(i, _):
            sp = pl.ds(pl.multiple_of(h * BLK + i * CH, CH), CH)
            tp = pl.ds(pl.multiple_of(row0 + i * CH, CH), CH)
            u, inv = moments(z.normed[sp, :] + z.acc[sp, :])
            pos = me * own + row0 + i * CH + iota((CH, 1), 0)
            valid = jnp.where(pos < n_valid, 1.0, 0.0)
            z.act[tp, :] = (u * g2 * valid).astype(bf16)
            gm = pull(z.cot[tp, :].astype(f32) * valid * g2, u, inv)
            z.acc[sp, :] = gm
            z.low[sp, :] = gm.astype(bf16)
            return 0

        lax.fori_loop(0, BLK // CH, norm_two, 0)
        ga = dot_nt(z.low[hs, :], z.wfo[0])
        for k in range(4):
            later = dot_nt(z.low[hs, :], z.wfo[k + 1]) if k < 3 else None
            z.acc[hs, :] += dot_nt((ga * z.gel[k, hs, :].astype(f32)).astype(bf16), z.wfi[k])
            ga = later

        def norm_back(i, _):
            sp = pl.ds(pl.multiple_of(h * BLK + i * CH, CH), CH)
            gm = pull(z.acc[sp, :] * g1, z.unit1[sp, :], z.inv1[sp, 0:1])
            z.normed[sp, :] = gm
            z.low[sp, :] = gm.astype(bf16)
            return 0

        lax.fori_loop(0, BLK // CH, norm_back, 0)
        later = dot_nt(z.low[hs, :], z.wout[0])
        for k in range(4):
            g = later
            if k < 3:
                later = dot_nt(z.low[hs, :], z.wout[k + 1])
            pair = g[:, 0:LANES].astype(bf16)
            last = jnp.where(left[0:HALF], g[0:HALF, LANES:], pltpu.roll(g[HALF:, LANES:], hd, 1)).astype(bf16)
            if k < 3:
                z.gsend[k, h, 0:BLK, :] = pair
                z.gsend[k, h, BLK:, :] = last
                grad_copy(k, h).start()
            else:
                z.grecv[me, h, 0:BLK, :] = pair
                z.grecv[me, h, BLK:, :] = last
        return 0

    lax.fori_loop(0, 2, rear, 0)

    z.adp[...] = jnp.zeros_like(z.adp)
    last_block = blocks - 1
    role = lax.rem(cc + yy, 2)

    def place(o):
        og = lax.div(o, 2)
        odd = lax.rem(o, 2)
        return (o + (last_block - 2 * o) * (1 - yy), og + (3 - 2 * og) * (1 - yy), odd + lax.div(o, 4) * (1 - 2 * odd))

    def peer_grad(o):
        return remote(z.gboth.at[o, :, 0:pack], z.gboth.at[o, :, pack:2 * pack], z.osem_s.at[o], z.osem_r.at[o], tensor_at(2))

    def part_copy(h):
        return remote(z.psend.at[h], z.precv.at[h], z.psem_s.at[h], z.psem_r.at[h], tensor_at(0))

    def finish(o):
        b, _, _ = place(o)
        span = span_of(b)
        scaled = 2 * width // LANES
        for c in range(pack // LANES):
            t = z.gt[c * LANES:(c + 1) * LANES, span].T
            z.gboth[o, :, c * LANES:(c + 1) * LANES] = (t * hd ** -0.5 if c < scaled else t).astype(bf16)
        z.adp[...] += 2.0 * dot(z.yt[3 * width:3 * width + 2 * rank, span], z.gboth[o, :, 0:pack])
        peer_grad(o).start()

    def contract(o):
        _, _, h = place(o)
        peer_grad(o).wait_recv()

        @pl.when(lax.rem(lax.div(o, 2) + role, 2) == 1)
        def _():
            both = dot(z.gboth[o], z.weff[...])

            @pl.when(o < 4)
            def _():
                z.psend[h] = both.astype(bf16)
                part_copy(h).start()

            @pl.when(o >= 4)
            def _():
                hs = span_of(h)
                z.normed[hs, :] = z.normed[hs, :] + both

    def back(n, _):
        @pl.when(n == 0)
        def _():
            grad_copy(0, 0).wait_recv()
            grad_copy(1, 0).wait_recv()

        @pl.when(n == 2)
        def _():
            grad_copy(0, 1).wait_recv()
            grad_copy(1, 1).wait_recv()
            grad_copy(2, 0).wait_recv()
            grad_copy(2, 1).wait_recv()

        d, m4 = lax.div(n, 4), lax.rem(n, 4)
        mid = lax.rem(lax.div(m4 + 1, 2), 2)
        o = n + (1 - d) * mid * (3 - 2 * n)
        qb, g, h2 = place(o)
        span = span_of(qb)

        def over(lo, count):
            pair_t = z.grecv[g, h2, 0:BLK, :].astype(f32).T
            last = z.grecv[g, h2, BLK:, :].astype(f32)
            last_t = jnp.concatenate([last, pltpu.roll(last, hd, 1)], axis=0).T[0:hd, :]
            for h in range(heads):
                do = last_t if h == 2 else pair_t[h * hd:(h + 1) * hd, :]
                z.dot_t[h * hd:(h + 1) * hd, :] = do.astype(bf16)
                delta = jnp.sum(do * z.ot[h * hd:(h + 1) * hd, span].astype(f32), axis=0, keepdims=True)
                tail = jnp.zeros((hd, BLK), f32)
                for j, p in enumerate(three_parts(-delta)):
                    tail = jnp.where(sub == j, p, tail)
                z.doa[h] = jnp.concatenate([do, tail], axis=0).T.astype(bf16)

            def scores(h, j):
                keys = span_of(lo + j)
                p = jnp.exp2(dot_nt(z.qa[h, span, :], z.ka[h, keys, :]) * LOG2E)
                z.pbuf[h, j] = p.astype(bf16)
                z.dsbuf[h, :, j * BLK:(j + 1) * BLK] = (p * dot_nt(z.doa[h], z.va[h, keys, :])).astype(bf16)

            for h in range(heads):
                scores(h, 0)
            for j in range(count):
                keys = span_of(lo + j)
                for h in range(heads):
                    rq = slice(h * hd, (h + 1) * hd)
                    rk = slice(width + h * hd, width + (h + 1) * hd)
                    rv = slice(2 * width + h * hd, 2 * width + (h + 1) * hd)
                    if j + 1 < count:
                        scores(h, j + 1)
                    z.gt[rv, keys] += dot(z.dot_t[rq, :], z.pbuf[h, j])
                    z.gt[rk, keys] += dot(z.yt[rq, span], z.dsbuf[h, :, j * BLK:(j + 1) * BLK])
                    if j + 1 == count:
                        around = pl.ds(pl.multiple_of(lo * BLK, BLK), count * BLK)
                        z.gt[rq, span] = dot_nt(z.yt[rk, around], z.dsbuf[h, :, 0:count * BLK])

            @pl.when(n >= 2)
            def _():
                finish(n - 2)

        low_edge = qb < REACH
        edge = low_edge | (qb >= blocks - REACH)
        few = min(2 * REACH, blocks)

        @pl.when(edge)
        def _():
            over(jnp.where(low_edge, 0, blocks - few), few)

        @pl.when(jnp.logical_not(edge))
        def _():
            over(window(qb), win)

        @pl.when(n == 3)
        def _():
            weff_out.wait_recv()

        @pl.when(n >= 3)
        def _():
            contract(n - 3)

        return 0

    lax.fori_loop(0, blocks, back, 0)

    def finish_loop(o, _):
        finish(o)
        return 0

    lax.fori_loop(blocks - 2, blocks, finish_loop, 0)
    wide = 2 * LANES
    z.asend[:, 0:wide] = z.adp[0:rank, 0:wide]
    z.asend[:, wide:] = z.adp[rank:, pack - wide:]
    adapters = [remote(z.asend, z.arecv.at[d], z.asem_s.at[d], z.asem_r.at[d], row_at(d)) for d in range(1, n_dp)]
    for c in adapters:
        c.start()

    def contract_loop(o, _):
        contract(o)
        return 0

    lax.fori_loop(blocks - 3, blocks, contract_loop, 0)
    for v in moves:
        for c in [v.a, v.x, v.z, v.far_x, v.far_z] + v.d:
            c.wait_send()
    for c in partners:
        c.wait_send()
    for h in range(2):
        part_copy(h).wait_recv()
        to = pl.ds(pl.multiple_of(my_rows(h), BLK), BLK)
        z.out[to, :] = z.normed[h * BLK:(h + 1) * BLK, :] + z.precv[h].astype(f32)
    total = z.asend[...]
    for c in adapters:
        c.wait_recv()
    for d in range(1, n_dp):
        total = total + z.arecv[d]
    cols = z.upq.shape[2]
    for base, ref in ((0, z.upq), (wide, z.upv)):
        for h in range(heads):
            at = base + h * hd
            tile = total[:, at // LANES * LANES:(at // LANES + 1) * LANES]
            ref[h] = pltpu.roll(tile, lax.rem(2 * LANES - at % LANES - dp * cols, LANES), 1)[:, 0:cols]

    weff_out.wait_send()
    for h in range(2):
        for k in range(3):
            ctx_copy(k, h).wait_send()
            grad_copy(k, h).wait_send()
        part_copy(h).wait_send()
    for o in range(blocks):
        peer_grad(o).wait_send()
    for c in adapters:
        c.wait_send()


def emit_kernel(act, out, upq, upv, act_hbm, out_hbm, upq_hbm, upv_hbm, sem):
    copies = [pltpu.make_async_copy(src, dst, sem.at[i]) for i, (src, dst) in
              enumerate(((out, out_hbm), (act, act_hbm), (upq, upq_hbm), (upv, upv_hbm)))]
    for c in copies:
        c.start()
    for c in copies:
        c.wait()


V = pl.BlockSpec(memory_space=pltpu.VMEM)
S = pl.BlockSpec(memory_space=pltpu.SMEM)
ANY = pl.BlockSpec(memory_space=pl.ANY)


def on_device(n_dp, groups, tokens, seq_lengths, query_weight, key_weight, value_weight, out_weight, ffn_in, ffn_out,
              gain_attn, gain_ffn, query_down, value_down, query_up, value_up, cotangent):
    rows, feat = tokens.shape
    width = query_weight.shape[1]
    rank, heads, hd = query_up.shape
    hidden = ffn_in.shape[1]
    own = rows // groups
    blocks = rows // BLK
    packed = (groups, own // BLK, BLK + HALF, LANES)
    pack = 5 * LANES
    cols = hd // n_dp
    win = min(2 * REACH + 1, blocks)
    dma = pltpu.SemaphoreType.DMA
    shape = jax.ShapeDtypeStruct
    inputs = [
        ("lens", seq_lengths, S), ("tok_hbm", tokens, ANY), ("cot_hbm", cotangent, ANY),
        ("wq", query_weight.T, V), ("wk", key_weight.T, V), ("wv", value_weight.T, V),
        ("dq", query_down.T, V), ("dv", value_down.T, V), ("uq", query_up.transpose(1, 0, 2), V), ("uv", value_up.transpose(1, 0, 2), V),
        ("ow", out_weight, ANY), ("fi", ffn_in, ANY), ("fo", ffn_out, ANY),
        ("g1", gain_attn.reshape(feat // LANES, LANES), V), ("g2", gain_ffn.reshape(feat // LANES, LANES), V),
    ]
    outputs = [
        ("act", shape((own, feat), bf16)), ("out", shape((own, feat), f32)),
        ("upq", shape((heads, rank, cols), f32)), ("upv", shape((heads, rank, cols), f32)),
    ]
    vm = pltpu.VMEM
    scratch = [
        ("tok", vm((rows, feat), bf16)), ("cot", vm((own, feat), bf16)),
        ("weff", vm((2 * pack, feat), bf16)),
        ("qa", vm((heads, rows, LANES), bf16)), ("ka", vm((heads, rows, LANES), bf16)), ("va", vm((heads, rows, LANES), bf16)),
        ("yt", vm((pack, rows), bf16)), ("vt", vm((heads, hd + 16, rows), bf16)), ("ot", vm((width, rows), bf16)),
        ("sbuf", vm((heads, win, BLK, BLK), f32)),
        ("xin", vm((BLK, groups * 2 * LANES), bf16)), ("xsend", vm(packed, bf16)), ("xb", vm(packed, bf16)),
        ("wout", vm((groups, 2 * LANES, feat), bf16)), ("wfi", vm((groups, feat, hidden), bf16)), ("wfo", vm((groups, hidden, feat), bf16)),
        ("normed", vm((own, feat), f32)), ("unit1", vm((own, feat), f32)), ("inv1", vm((own, LANES), f32)),
        ("low", vm((own, feat), bf16)), ("acc", vm((own, feat), f32)), ("gel", vm((groups, own, hidden), bf16)),
        ("actv", vm((2, BLK, hidden), bf16)), ("gsend", vm(packed, bf16)), ("grecv", vm(packed, bf16)),
        ("doa", vm((heads, BLK, LANES), bf16)), ("dot_t", vm((width, BLK), bf16)),
        ("pbuf", vm((heads, win, BLK, BLK), bf16)), ("dsbuf", vm((heads, BLK, win * BLK), bf16)),
        ("gt", vm((pack, rows), f32)), ("adp", vm((2 * rank, pack), f32)),
        ("gboth", vm((blocks, BLK, 2 * pack), bf16)),
        ("psend", vm((2, BLK, feat), bf16)), ("precv", vm((2, BLK, feat), bf16)),
        ("asend", vm((rank, 4 * LANES), f32)), ("arecv", vm((n_dp, rank, 4 * LANES), f32)),
        ("lsem", dma((8,))), ("wsem_s", dma((5, 9))), ("wsem_r", dma((5, 9))), ("bsem_s", dma((3,))), ("bsem_r", dma((3,))), ("esem_s", dma((1,))), ("esem_r", dma((1,))),
        ("csem_s", dma((3, 2))), ("csem_r", dma((3, 2))), ("gsem_s", dma((3, 2))), ("gsem_r", dma((3, 2))),
        ("osem_s", dma((blocks,))), ("osem_r", dma((blocks,))), ("psem_s", dma((2,))), ("psem_r", dma((2,))),
        ("asem_s", dma((n_dp,))), ("asem_r", dma((n_dp,))),
    ]
    names = [n for n, _, _ in inputs] + [n for n, _ in outputs] + [n for n, _ in scratch]
    results = pl.pallas_call(
        functools.partial(layer_kernel, n_dp, heads, hd, names),
        out_shape=tuple(vm(s.shape, s.dtype) for _, s in outputs),
        in_specs=[s for _, _, s in inputs],
        out_specs=(V,) * 4,
        scratch_shapes=[s for _, s in scratch],
        compiler_params=pltpu.CompilerParams(vmem_limit_bytes=VMEM_LIMIT, collective_id=0, has_side_effects=True),
        name="layer",
    )(*[a for _, a, _ in inputs])
    act, grad_input, up_q, up_v = pl.pallas_call(
        emit_kernel,
        out_shape=tuple(s for _, s in outputs),
        in_specs=[V] * 4,
        out_specs=(ANY,) * 4,
        scratch_shapes=[dma((4,))],
        compiler_params=pltpu.CompilerParams(vmem_limit_bytes=4 * 1024 * 1024),
        name="emit",
    )(*results)
    return act, grad_input, up_q.transpose(1, 0, 2), up_v.transpose(1, 0, 2)


def solution(mesh):
    in_specs = (
        P("dp", None), P("dp", None), P(None, "tensor"), P(None, "tensor"), P(None, "tensor"), P("tensor", None),
        P(None, "tensor"), P("tensor", None), P(), P(), P(), P(), P(None, "tensor", None), P(None, "tensor", None),
        P("dp", None),
    )
    out_specs = (P(("dp", "tensor"), None), P(("dp", "tensor"), None), P(None, "tensor", "dp"), P(None, "tensor", "dp"))
    return jax.shard_map(
        functools.partial(on_device, mesh.shape["dp"], mesh.shape["tensor"]),
        mesh=mesh, in_specs=in_specs, out_specs=out_specs, check_vma=False,
    )
```
